32 devices in a mesh: lon: 8 (over z, x), lat: 4 (over y, core).
Axes of the slice: x: 2, y: 2, z: 4, core: 2. Of those that a mesh axis runs over, the one named last changes fastest.
Arguments:
- field: float32 [2, 128, 512], P(None, 'lat', 'lon'), may hold values from -6 to 6
- gamma: float32 [2, 128, 512], P(None, 'lat', 'lon'), may hold values from 1 to 192
- kappa_zonal: float32 [2, 128, 512], P(None, 'lat', 'lon'), may hold values from 4096 to 49152
- kappa_merid: float32 [2, 128, 512], P(None, 'lat', 'lon'), may hold values from 1024 to 12288
- area: float32 [128, 512], P('lat', 'lon'), may hold values from 0.3 to 3
- sea_mask: int32 [128, 512], P('lat', 'lon'), may hold values from 0 to 1, as said below
- fold_pair: int32 [512], P('lon'), may hold values from 0 to 511, as said below
Outputs:
- covaried: float32 [2, 128, 512], P(None, 'lat', 'lon')
The draws below stay inside these ranges and needn't reach their ends.
Inputs may be any that keep to these rules, and one draw needn't show every extreme that they name: `sea_mask`: ocean cells are 1 and land cells 0; land comes in rectangles, periodic in longitude. A mirror pairing across the fold: fold_pair[i] + i is the same odd number modulo 512 for every i, so fold_pair[fold_pair[i]] == i and fold_pair[i] != i.
All inputs are finite; a program needn't handle non-finite values.
Results may differ from the reference program's by a relative error of at most 0.00095.
Values sent between devices are 32-bit elements; how exact they have to be, the bound alone decides.
No kernel may reach another device: no remote copies, remote signals or barrier semaphores. Data moves between devices by JAX's collectives and lax.ppermute only.
A program may use at most 64 MiB of HBM per device.

```python
import math
import jax
import jax.numpy as jnp
from jax import lax

LEV = 2
CY = 32
CX = 64
NX = 512
NY = 128


def draw_sea_mask(key, part):
    count = 12
    keys = jax.random.split(jax.random.fold_in(key, 7), 4)
    left = jax.random.randint(keys[0], (count,), 0, NX)
    widths = jax.random.randint(keys[1], (count,), NX // 16 + 1, NX // 5 + 2)
    bottom = jax.random.randint(keys[2], (count,), 0, NY - NY // 8)
    heights = jax.random.randint(keys[3], (count,), NY // 16 + 1, NY // 4 + 2)
    columns = jnp.arange(NX, dtype=jnp.int32)[None, :]
    rows_index = jnp.arange(NY, dtype=jnp.int32)[:, None]

    def add_land(which, land):
        inside_x = (columns - left[which]) % NX < widths[which]
        inside_y = (rows_index >= bottom[which]) & (rows_index < bottom[which] + heights[which])
        return jnp.maximum(land, (inside_x & inside_y).astype(jnp.int32))
    land = lax.fori_loop(0, count, add_land, jnp.zeros((NY, NX), jnp.int32))
    return (1 - land).astype(jnp.int32)


def draw_fold_pair(key, part):
    half_count = NX // 2
    pivot_sum = 2 * jax.random.randint(jax.random.fold_in(key, 11), (), 0, half_count) + 1
    columns = jnp.arange(NX, dtype=jnp.int32)
    return ((pivot_sum - columns) % NX).astype(jnp.int32)


def draw_field(key, part):
    shape = (LEV, NY, NX)
    subkey = jax.random.fold_in(key, 21)
    return jnp.clip(jax.random.normal(subkey, shape, jnp.float32), -6.0, 6.0)


def draw_gamma(key, part):
    shape = (LEV, NY, NX)
    subkey = jax.random.fold_in(key, 22)
    base = math.sqrt(3.0 * (CX + CY))
    exponent = jax.random.uniform(subkey, shape, jnp.float32, -1.15, 1.15)
    return (base * jnp.exp(exponent)).astype(jnp.float32)


def diffusivity(key, constant, block_width):
    shape = (LEV, NY, NX)
    subkey = jax.random.fold_in(key, constant)
    square = float(block_width * block_width)
    exponent = jax.random.uniform(subkey, shape, jnp.float32, 0.0, math.log(9.0))
    return (square * jnp.exp(exponent)).astype(jnp.float32)


def draw_kappa_zonal(key, part):
    return diffusivity(key, 23, CX)


def draw_kappa_merid(key, part):
    return diffusivity(key, 24, CY)


def level_of(stream_key, dims, shards, least, high):
    gain = 1.0
    for dim, parts in shards:
        steps = jax.random.uniform(jax.random.fold_in(jax.random.fold_in(stream_key, 6), dim), (parts,), jnp.float32, least / len(shards), high / len(shards))
        gain = gain * jnp.repeat(jnp.exp(steps), dims[dim] // parts).reshape((-1,) + (1,) * (len(dims) - 1 - dim))
    return gain


def setup_inputs(seed: int = 0) -> dict:
    seeds = jax.random.split(jax.random.key(seed), 8)
    return {
        "field": draw_field(jax.random.fold_in(seeds[7], 71), 0),
        "gamma": draw_gamma(jax.random.fold_in(seeds[7], 71), 0),
        "kappa_zonal": draw_kappa_zonal(jax.random.fold_in(seeds[7], 71), 0),
        "kappa_merid": draw_kappa_merid(jax.random.fold_in(seeds[7], 71), 0),
        "area": jnp.clip(jnp.exp(math.log(3.0) - 2.3025851 * jax.random.uniform(seeds[4], (NY, NX), jnp.float32) ** level_of(seeds[4], (NY, NX), ((0, 4), (1, 8)), -0.2, 0.2)), 0.3, 3.0),
        "sea_mask": draw_sea_mask(jax.random.fold_in(seeds[7], 71), 0),
        "fold_pair": draw_fold_pair(jax.random.fold_in(seeds[7], 71), 0),
    }


def cyclic_solve(faces, source):
    length = source.shape[-1]
    before = jnp.roll(faces, 1, axis=-1)
    diagonal = 1.0 + before + faces
    column = lax.broadcasted_iota(jnp.int32, source.shape, source.ndim - 1)
    first_cell = column == 0
    last_cell = column == length - 1
    corner = -faces[..., -1:]
    pivot_value = -diagonal[..., :1]
    lower_band = jnp.where(first_cell, 0.0, -before)
    upper_band = jnp.where(last_cell, 0.0, -faces)
    shifted = diagonal - jnp.where(first_cell, pivot_value, 0.0) - jnp.where(last_cell, corner * corner / pivot_value, 0.0)
    column_bump = jnp.where(first_cell, pivot_value, 0.0) + jnp.where(last_cell, corner, 0.0)
    solved = lax.linalg.tridiagonal_solve(lower_band, shifted, upper_band, jnp.stack([source, column_bump], -1))
    direct = solved[..., 0]
    spread = solved[..., 1]
    numerator = direct[..., :1] + corner / pivot_value * direct[..., -1:]
    denominator = 1.0 + spread[..., :1] + corner / pivot_value * spread[..., -1:]
    return direct - numerator / denominator * spread

def open_solve(faces, source):
    before = jnp.concatenate([jnp.zeros_like(faces[..., :1]), faces[..., :-1]], axis=-1)
    diagonal = 1.0 + before + faces
    column = lax.broadcasted_iota(jnp.int32, source.shape, source.ndim - 1)
    upper_band = jnp.where(column == source.shape[-1] - 1, 0.0, -faces)
    solved = lax.linalg.tridiagonal_solve(-before, diagonal, upper_band, source[..., None])
    return solved[..., 0]

def merid_solve(faces, source):
    return jnp.swapaxes(open_solve(jnp.swapaxes(faces, 1, 2), jnp.swapaxes(source, 1, 2)), 1, 2)

def fold_rows(current, pairing):
    top_cells = current[:, -1, :]
    partner = jnp.take(top_cells, pairing, axis=1)
    return current.at[:, -1, :].set(0.5 * (top_cells + partner))

def reference(field, gamma, kappa_zonal, kappa_merid, area, sea_mask, fold_pair):
    ocean_cells = sea_mask.astype(jnp.float32)
    east_ocean = jnp.roll(ocean_cells, -1, axis=1)
    north_ocean = jnp.concatenate([ocean_cells[1:], jnp.zeros_like(ocean_cells[:1])], axis=0)
    zonal_faces = kappa_zonal * (ocean_cells * east_ocean)[None]
    merid_faces = kappa_merid * (ocean_cells * north_ocean)[None]
    scaled = gamma * ocean_cells[None]
    current = cyclic_solve(zonal_faces, scaled * field)
    current = merid_solve(merid_faces, current)
    current = fold_rows(current, fold_pair)
    current = current / area[None]
    current = fold_rows(current, fold_pair)
    current = merid_solve(merid_faces, current)
    current = cyclic_solve(zonal_faces, current)
    return scaled * current
```

```python
import functools

import jax
import jax.numpy as jnp
from jax import lax
from jax.experimental import pallas as pl
from jax.experimental.pallas import tpu as pltpu
from jax.sharding import PartitionSpec as P


F32 = jnp.float32
EXACT = lax.Precision.HIGHEST


def moved(values, distance, axis):
    return pltpu.roll(values, distance % values.shape[axis], axis)


def iota(shape, axis):
    return lax.broadcasted_iota(jnp.int32, shape, axis)


def spread(values, up, down, stride, axis):
    return values + moved(up * values, stride, axis) + moved(down * values, -stride, axis)


def condense(left, right, totals, count, axis):
    factors = []
    stride = 1
    while stride < count:
        pull = 1.0 / (totals[0] + left + right)
        up, down = right * pull, left * pull
        link = left * up
        factors.append((up, down))
        totals = [spread(t, up, down, stride, axis) for t in totals]
        left, right = moved(link, stride, axis), moved(link, -stride, axis)
        stride *= 2
    return factors, totals


def relax(values, factors, axis):
    stride = 1
    for up, down in factors:
        values = spread(values, up, down, stride, axis)
        stride *= 2
    return values


def load_factors(ref):
    return [(ref[2 * k], ref[2 * k + 1]) for k in range(ref.shape[0] // 2)]


def store_factors(ref, factors):
    for k, (up, down) in enumerate(factors):
        ref[2 * k] = up
        ref[2 * k + 1] = down


def beside(ref):
    return jnp.concatenate([ref[k] for k in range(ref.shape[0])], axis=-1)


def chain(faces, place, length, axis):
    inner = (place >= 1) & (place <= length - 3)
    right = jnp.where(inner, faces, 0.0)
    left = moved(right, 1, axis)
    to_first = jnp.where(place == 1, moved(faces, 1, axis), 0.0)
    to_last = jnp.where(place == length - 2, faces, 0.0)
    return left, right, to_first, to_last


def half_sums(arrays, levels):
    wide = jnp.concatenate(arrays, axis=1)
    lanes = arrays[0].shape[1]
    width = lanes // levels
    shape = (8 * levels, wide.shape[1])
    row, col = iota(shape, 0), iota(shape, 1)
    pick = ((col // lanes == row % 8) & (col % lanes // width == row // 8)).astype(F32)
    sums = lax.dot_general(pick, wide, (((1,), (1,)), ((), ())), precision=EXACT, preferred_element_type=F32)
    return jnp.concatenate([sums[8 * k : 8 * k + 8] for k in range(levels)], axis=1)


def padded(rows, lanes):
    return jnp.concatenate([rows, jnp.zeros((rows.shape[0], lanes - rows.shape[1]), F32)], axis=1)


def zonal_local(field, gamma, kappa, mask, message, factors_out, out):
    levels, height, width = field.shape
    ocean = mask[...].astype(F32)
    ocean = jnp.concatenate([ocean] * levels, axis=1)
    lanes = levels * width
    place = iota((height, lanes), 1) % width
    scaled = beside(gamma) * ocean
    source = scaled * beside(field)
    open_face = beside(kappa) * ocean
    faces = open_face * moved(ocean, -1, 1)
    left, right, to_first, to_last = chain(faces, place, width, 1)
    factors, (ground, first, last) = condense(
        left, right, [1.0 + to_first + to_last, to_first, to_last], width - 2, 1
    )
    inverse = 1.0 / ground
    first = first * inverse
    last = last * inverse
    edge = to_first * last
    first_full = jnp.where(place == 0, 1.0, first)
    last_full = jnp.where(place == width - 1, 1.0, last)
    rows = half_sums(
        [
            first_full * source,
            last_full * source,
            first_full,
            last_full,
            edge,
            jnp.where(place == width - 1, open_face, 0.0),
            jnp.where(place == 0, ocean, 0.0),
        ],
        levels,
    )
    message[...] = jnp.broadcast_to(padded(rows, message.shape[2])[None], message.shape)
    store_factors(factors_out, factors)
    inner = (place >= 1) & (place <= width - 2)
    out[0] = first_full
    out[1] = last_full
    out[2] = jnp.where(inner, inverse, 0.0)
    out[3] = source
    out[4] = scaled


def merid_local(zonal_factors, zonal, kappa, area, mask, direct, factors_out, out, rows_out):
    levels, height, width = kappa.shape
    ocean = mask[...].astype(F32)
    ocean = jnp.concatenate([ocean] * levels, axis=1)
    reciprocal = 1.0 / area[...]
    reciprocal = jnp.concatenate([reciprocal] * levels, axis=1)
    lanes = levels * width
    row = iota((height, lanes), 0)
    open_face = beside(kappa) * ocean
    faces = open_face * moved(ocean, -1, 0)
    left, right, to_first, to_last = chain(faces, row, height, 0)
    factors, (ground, first, last) = condense(
        left, right, [1.0 + to_first + to_last, to_first, to_last], height - 2, 0
    )
    inner = (row >= 1) & (row <= height - 2)
    inverse = jnp.where(inner, 1.0 / ground, 0.0)
    first = first * inverse
    last = last * inverse
    edge = jnp.sum(to_first * last, axis=0, keepdims=True)
    again_first = relax(first * reciprocal, factors, 0) * inverse
    again_last = relax(last * reciprocal, factors, 0) * inverse
    first = jnp.where(row == 0, 1.0, first)
    last = jnp.where(row == height - 1, 1.0, last)

    def total(values):
        return jnp.sum(values, axis=0, keepdims=True)

    rows = [
        total(first),
        total(last),
        edge,
        open_face[height - 1 :],
        ocean[:1],
        total(first * first * reciprocal),
        total(first * last * reciprocal),
        total(jnp.where(row == height - 1, 0.0, last * last * reciprocal)),
        reciprocal[height - 1 :],
    ]
    rows_out[...] = jnp.concatenate([jnp.zeros((4, lanes), F32)] + rows + [jnp.zeros((3, lanes), F32)], axis=0)
    store_factors(factors_out, factors)
    out[0] = first
    out[1] = last
    out[2] = again_first
    out[3] = again_last
    out[4] = inverse
    out[5] = reciprocal
    direct[...] = relax(zonal[3] * (zonal[2] > 0.0), load_factors(zonal_factors), 1) * zonal[2]


def own_columns(values, index, height, levels, lanes):
    own = jnp.sum(jnp.where(iota(values.shape, 0) == index, values, 0.0), axis=0, keepdims=True)
    shape = (height, values.shape[1])
    row, col = iota(shape, 0), iota(shape, 1)
    columns = [
        jnp.sum(jnp.where(col == row + k * height, own, 0.0), axis=1, keepdims=True) for k in range(levels)
    ]
    lane = iota((height, lanes), 1)
    width = lanes // levels
    result = jnp.broadcast_to(columns[0], (height, lanes))
    for k in range(1, levels):
        result = jnp.where(lane >= k * width, columns[k], result)
    return result


def ring_ends(first_source, last_source, edge_pull, face_pull, last_pull, factors, inverse):
    values = first_source + edge_pull * last_source + moved(face_pull * last_source, 1, 0)
    first = relax(values, factors, 0) * inverse
    last = last_pull * last_source + edge_pull * first + face_pull * moved(first, -1, 0)
    return first, last


def zonal_join(gathered, zonal, direct, merid, merid_rows, current_out, message, ring):
    levels = 2
    height, lanes = direct.shape
    index = lax.axis_index("lon")
    first_source, last_source, first_ground, last_ground, edge, open_face, ocean = [
        gathered[:, k, :] for k in range(7)
    ]
    devices = edge.shape[0]
    used = iota(edge.shape, 1) < levels * height
    first_ground = jnp.where(used, first_ground, 1.0)
    last_ground = jnp.where(used, last_ground, 1.0)
    face = open_face * moved(ocean, -1, 0)
    last_pull = 1.0 / (last_ground + edge + face)
    edge_pull, face_pull = edge * last_pull, face * last_pull
    ground = first_ground + edge_pull * last_ground + moved(face_pull * last_ground, 1, 0)
    link = edge * face_pull
    factors, (ground,) = condense(moved(link, 1, 0), link, [ground], devices, 0)
    inverse = 1.0 / ground
    first, last = ring_ends(first_source, last_source, edge_pull, face_pull, last_pull, factors, inverse)
    ring[0] = edge_pull
    ring[1] = face_pull
    ring[2] = last_pull
    ring[3] = inverse
    for k, (up, down) in enumerate(factors):
        ring[4 + 2 * k] = up
        ring[5 + 2 * k] = down
    current = (
        direct[...]
        + zonal[0] * own_columns(first, index, height, levels, lanes)
        + zonal[1] * own_columns(last, index, height, levels, lanes)
    )
    current_out[...] = current
    rows = [jnp.sum(merid[k] * current, axis=0, keepdims=True) for k in range(4)]
    whole = jnp.concatenate(rows + [merid_rows[4:]], axis=0)
    message[...] = jnp.broadcast_to(whole[None], message.shape)


def merid_twice(current, factors_ref, merid, out):
    factors = load_factors(factors_ref)
    inner = merid[4] > 0.0
    once = relax(jnp.where(inner, current[...], 0.0), factors, 0) * merid[4]
    out[...] = relax(once * merid[5], factors, 0) * merid[4]


def line_factors(left, right, ground):
    count = len(ground)
    factors = []
    stride = 1
    while stride < count:
        pull = [1.0 / (ground[k] + left[k] + right[k]) for k in range(count)]
        up = [right[k] * pull[k] for k in range(count)]
        down = [left[k] * pull[k] for k in range(count)]
        link = [left[k] * up[k] for k in range(count)]
        factors.append((up, down))
        ground = line_relax(ground, [factors[-1]], stride)
        zero = jnp.zeros_like(link[0])
        left = [link[k - stride] if k >= stride else zero for k in range(count)]
        right = [link[k + stride] if k + stride < count else zero for k in range(count)]
        stride *= 2
    return factors, ground


def line_relax(values, factors, stride=1):
    count = len(values)
    for up, down in factors:
        fresh = []
        for k in range(count):
            value = values[k]
            if k >= stride:
                value = value + up[k - stride] * values[k - stride]
            if k + stride < count:
                value = value + down[k + stride] * values[k + stride]
            fresh.append(value)
        values = fresh
        stride *= 2
    return values


def mirrored(values, pivot, width, levels):
    count, devices, lanes = values.shape
    pivot_block, pivot_place = pivot // width, pivot % width
    shape = (lanes, lanes)
    source, target = iota(shape, 0), iota(shape, 1)
    reach = pivot_place - target % width
    same = source // width == target // width
    flat = values.reshape(count * devices, lanes)
    result = 0.0
    for extra in range(2):
        lane_pick = (same & (source % width == reach + extra * width)).astype(F32)
        turned = lax.dot(flat, lane_pick, precision=EXACT, preferred_element_type=F32)
        shape = (count * devices, count * devices)
        goal, origin = iota(shape, 0), iota(shape, 1)
        wanted = (pivot_block - goal % devices - extra + 2 * devices) % devices
        block_pick = ((goal // devices == origin // devices) & (origin % devices == wanted)).astype(F32)
        result = result + lax.dot(block_pick, turned, precision=EXACT, preferred_element_type=F32)
    return result.reshape(values.shape)


def merid_join(gathered, again, merid, zonal, pairing, current_out, message):
    levels = 2
    height, lanes = again.shape
    width = lanes // levels
    devices_x, devices_y = gathered.shape[:2]
    index_x, index_y = lax.axis_index("lon"), lax.axis_index("lat")
    pivot = (pairing[0] + index_x * width) % (devices_x * width)

    def part(k):
        return [gathered[:, y, k, :] for y in range(devices_y)]

    (first_source, last_source, first_again, last_again, first_ground, last_ground, edge, open_face, ocean,
     first_first, first_last, last_last, reciprocal) = [part(k) for k in range(13)]
    lats = range(devices_y)
    top = devices_y - 1
    face = [open_face[y] * ocean[y + 1] if y < top else jnp.zeros_like(edge[y]) for y in lats]
    last_pull = [1.0 / (last_ground[y] + edge[y] + face[y]) for y in lats]
    edge_pull = [edge[y] * last_pull[y] for y in lats]
    face_pull = [face[y] * last_pull[y] for y in lats]
    below = lambda values: [values[y - 1] if y > 0 else jnp.zeros_like(values[0]) for y in lats]

    def gather_to_first(first_values, last_values):
        up = below([face_pull[y] * last_values[y] for y in lats])
        return [first_values[y] + edge_pull[y] * last_values[y] + up[y] for y in lats]

    link = [edge[y] * face_pull[y] for y in lats]
    factors, ground = line_factors(below(link), link, gather_to_first(first_ground, last_ground))
    inverse = [1.0 / g for g in ground]

    def ends(first_values, last_values):
        relaxed = line_relax(gather_to_first(first_values, last_values), factors)
        first = [relaxed[y] * inverse[y] for y in lats]
        last = []
        for y in lats:
            value = last_pull[y] * last_values[y] + edge_pull[y] * first[y]
            if y < top:
                value = value + face_pull[y] * first[y + 1]
            last.append(value)
        return first, last

    first_one, last_one = ends(first_source, last_source)
    across = mirrored(jnp.stack([last_one[top], reciprocal[top]]), pivot, width, levels)
    folded = 0.25 * (last_one[top] + across[0]) * (reciprocal[top] + across[1])
    first_next = [
        first_again[y] + first_first[y] * first_one[y] + first_last[y] * last_one[y] for y in lats
    ]
    last_next = [
        last_again[y]
        + first_last[y] * first_one[y]
        + last_last[y] * last_one[y]
        + (reciprocal[y] * last_one[y] if y < top else folded)
        for y in lats
    ]
    first_two, last_two = ends(first_next, last_next)

    def own(values):
        chosen = values[0]
        for y in range(1, devices_y):
            chosen = jnp.where(index_y == y, values[y], chosen)
        return jnp.sum(jnp.where(iota(chosen.shape, 0) == index_x, chosen, 0.0), axis=0, keepdims=True)

    current = (
        again[...]
        + merid[2] * own(first_one)
        + merid[3] * own(last_one)
        + merid[0] * own(first_two)
        + merid[1] * own(last_two)
    )
    current_out[...] = current
    rows = half_sums([zonal[0] * current, zonal[1] * current], levels)
    message[...] = jnp.broadcast_to(padded(rows, message.shape[2])[None], message.shape)


def zonal_again(factors_ref, zonal, current, out):
    out[...] = relax(current[...] * (zonal[2] > 0.0), load_factors(factors_ref), 1) * zonal[2]


def zonal_close(gathered, ring, zonal, direct, out):
    levels, height, width = out.shape
    lanes = levels * width
    index = lax.axis_index("lon")
    factors = [(ring[4 + 2 * k], ring[5 + 2 * k]) for k in range((ring.shape[0] - 4) // 2)]
    first, last = ring_ends(gathered[:, 0, :], gathered[:, 1, :], ring[0], ring[1], ring[2], factors, ring[3])
    result = zonal[4] * (
        direct[...]
        + zonal[0] * own_columns(first, index, height, levels, lanes)
        + zonal[1] * own_columns(last, index, height, levels, lanes)
    )
    for k in range(levels):
        out[k] = result[:, k * width : (k + 1) * width]


def run(body, shapes, *operands, scalars=()):
    vmem = pl.BlockSpec(memory_space=pltpu.VMEM)
    smem = pl.BlockSpec(memory_space=pltpu.SMEM)
    return pl.pallas_call(
        body,
        out_shape=[jax.ShapeDtypeStruct(shape, F32) for shape in shapes],
        in_specs=[smem if k in scalars else vmem for k in range(len(operands))],
        out_specs=[vmem] * len(shapes),
        name=body.__name__,
    )(*operands)


def steps(count):
    return (count - 1).bit_length()


def to_all(message, axis):
    return lax.all_to_all(message, axis, split_axis=0, concat_axis=0, tiled=True)


def local(field, gamma, kappa_zonal, kappa_merid, area, sea_mask, fold_pair):
    levels, height, width = field.shape
    lanes = levels * width
    devices_x, devices_y = lax.axis_size("lon"), lax.axis_size("lat")
    tile = (height, lanes)
    zonal_count, merid_count = 2 * steps(width - 2), 2 * steps(height - 2)

    message, zonal_factors, zonal = run(
        zonal_local,
        [(devices_x, 8, lanes), (zonal_count,) + tile, (5,) + tile],
        field, gamma, kappa_zonal, sea_mask,
    )
    gathered = to_all(message, "lon")
    direct, merid_factors, merid, merid_rows = run(
        merid_local,
        [tile, (merid_count,) + tile, (6,) + tile, (16, lanes)],
        zonal_factors, zonal, kappa_merid, area, sea_mask,
    )
    current, message, ring = run(
        zonal_join,
        [tile, (devices_x * devices_y, 16, lanes), (4 + 2 * steps(devices_x), devices_x, lanes)],
        gathered, zonal, direct, merid, merid_rows,
    )
    gathered = to_all(message, ("lon", "lat")).reshape(devices_x, devices_y, 16, lanes)
    (again,) = run(merid_twice, [tile], current, merid_factors, merid)
    current, message = run(
        merid_join, [tile, (devices_x, 8, lanes)], gathered, again, merid, zonal, fold_pair, scalars=(4,)
    )
    gathered = to_all(message, "lon")
    (direct,) = run(zonal_again, [tile], zonal_factors, zonal, current)
    (result,) = run(zonal_close, [(levels, height, width)], gathered, ring, zonal, direct)
    return result


def solution(mesh):
    blocks = P(None, "lat", "lon")
    return jax.shard_map(
        local,
        mesh=mesh,
        in_specs=(blocks, blocks, blocks, blocks, P("lat", "lon"), P("lat", "lon"), P("lon")),
        out_specs=blocks,
        check_vma=False,
    )
```

```python
import functools

import jax
import jax.numpy as jnp
from jax import lax
from jax.experimental import pallas as pl
from jax.experimental.pallas import tpu as pltpu
from jax.sharding import PartitionSpec as P


F32 = jnp.float32
EXACT = lax.Precision.HIGHEST


def moved(values, distance, axis):
    return pltpu.roll(values, distance % values.shape[axis], axis)


def iota(shape, axis):
    return lax.broadcasted_iota(jnp.int32, shape, axis)


def spread(values, up, down, stride, axis):
    return values + moved(up * values, stride, axis) + moved(down * values, -stride, axis)


def condense(left, right, totals, count, axis):
    factors = []
    stride = 1
    while stride < count:
        pull = 1.0 / (totals[0] + left + right)
        up, down = right * pull, left * pull
        link = left * up
        factors.append((up, down))
        totals = [spread(t, up, down, stride, axis) for t in totals]
        left, right = moved(link, stride, axis), moved(link, -stride, axis)
        stride *= 2
    return factors, totals


def relax(values, factors, axis):
    stride = 1
    for up, down in factors:
        values = spread(values, up, down, stride, axis)
        stride *= 2
    return values


def load_factors(ref):
    return [(ref[2 * k], ref[2 * k + 1]) for k in range(ref.shape[0] // 2)]


def store_factors(ref, factors):
    for k, (up, down) in enumerate(factors):
        ref[2 * k] = up
        ref[2 * k + 1] = down


def beside(ref):
    return jnp.concatenate([ref[k] for k in range(ref.shape[0])], axis=-1)


def chain(faces, place, length, axis):
    inner = (place >= 1) & (place <= length - 3)
    right = jnp.where(inner, faces, 0.0)
    left = moved(right, 1, axis)
    to_first = jnp.where(place == 1, moved(faces, 1, axis), 0.0)
    to_last = jnp.where(place == length - 2, faces, 0.0)
    return left, right, to_first, to_last


def half_sums(arrays, levels):
    wide = jnp.concatenate(arrays, axis=1)
    lanes = arrays[0].shape[1]
    width = lanes // levels
    shape = (8 * levels, wide.shape[1])
    row, col = iota(shape, 0), iota(shape, 1)
    pick = ((col // lanes == row % 8) & (col % lanes // width == row // 8)).astype(F32)
    sums = lax.dot_general(pick, wide, (((1,), (1,)), ((), ())), precision=EXACT, preferred_element_type=F32)
    return jnp.concatenate([sums[8 * k : 8 * k + 8] for k in range(levels)], axis=1)


def padded(rows, lanes):
    return jnp.concatenate([rows, jnp.zeros((rows.shape[0], lanes - rows.shape[1]), F32)], axis=1)


def fetch(sources, buffers, semaphores):
    copies = [
        pltpu.make_async_copy(source, buffer, semaphores.at[k])
        for k, (source, buffer) in enumerate(zip(sources, buffers))
    ]
    for copy in copies:
        copy.start()
    for copy in copies:
        copy.wait()


def block_local(*refs):
    sources, (message, payload, factors_out, keep), buffers, semaphores = refs[:6], refs[6:10], refs[10:16], refs[16]
    fetch(sources, buffers, semaphores)
    field, gamma, kappa_zonal, kappa_merid, area, mask = buffers
    levels, height, width = field.shape
    lanes = levels * width
    ocean_one = mask[...].astype(F32)
    ocean = jnp.concatenate([ocean_one] * levels, axis=1)
    place = iota((height, lanes), 1) % width
    scaled = beside(gamma) * ocean
    source = scaled * beside(field)
    open_face = beside(kappa_zonal) * ocean
    faces = open_face * moved(ocean, -1, 1)
    left, right, to_first, to_last = chain(faces, place, width, 1)
    inner = (place >= 1) & (place <= width - 2)
    factors, (ground, first, last, direct) = condense(
        left,
        right,
        [1.0 + to_first + to_last, to_first, to_last, jnp.where(inner, source, 0.0)],
        width - 2,
        1,
    )
    inverse = jnp.where(inner, 1.0 / ground, 0.0)
    first = first * inverse
    last = last * inverse
    edge = to_first * last
    first = jnp.where(place == 0, 1.0, first)
    last = jnp.where(place == width - 1, 1.0, last)
    rows = half_sums(
        [
            first * source,
            last * source,
            first,
            last,
            edge,
            jnp.where(place == width - 1, open_face, 0.0),
            jnp.where(place == 0, ocean, 0.0),
        ],
        levels,
    )
    message[...] = jnp.broadcast_to(jnp.concatenate([rows[:4], rows[4:]], axis=1)[None], message.shape)
    payload[0] = direct * inverse
    payload[1] = first
    payload[2] = last
    payload[3] = beside(kappa_merid) * ocean
    payload[4] = jnp.concatenate([1.0 / area[...], ocean_one], axis=1)
    store_factors(factors_out, factors)
    keep[0] = first
    keep[1] = last
    keep[2] = inverse
    keep[3] = scaled


def ring_setup(first_ground, last_ground, edge, open_face, ocean):
    face = open_face * moved(ocean, -1, 0)
    last_pull = 1.0 / (last_ground + edge + face)
    edge_pull, face_pull = edge * last_pull, face * last_pull
    ground = first_ground + edge_pull * last_ground + moved(face_pull * last_ground, 1, 0)
    link = edge * face_pull
    factors, (ground,) = condense(moved(link, 1, 0), link, [ground], edge.shape[0], 0)
    return edge_pull, face_pull, last_pull, factors, 1.0 / ground


def ring_ends(first_source, last_source, edge_pull, face_pull, last_pull, factors, inverse):
    values = first_source + edge_pull * last_source + moved(face_pull * last_source, 1, 0)
    first = relax(values, factors, 0) * inverse
    last = last_pull * last_source + edge_pull * first + face_pull * moved(first, -1, 0)
    return first, last


def own_row(values, index):
    return jnp.sum(jnp.where(iota(values.shape, 0) == index, values, 0.0), axis=0, keepdims=True)


def columns(own, block, height, levels, lanes):
    width = lanes // levels
    row, col = iota((height, lanes), 0), iota((height, lanes), 1)
    result = None
    for k in range(levels):
        base = (block * levels + k) * height
        group = own[:, base // lanes * lanes : base // lanes * lanes + lanes]
        column = jnp.sum(jnp.where(col == row + base % lanes, group, 0.0), axis=1, keepdims=True)
        result = jnp.broadcast_to(column, (height, lanes)) if k == 0 else jnp.where(col >= k * width, column, result)
    return result


def column_join(gathered, payload, keep, kept, message):
    levels = 2
    devices_y, _, height, lanes = payload.shape
    lines = levels * height
    index_x, index_y = lax.axis_index("lon"), lax.axis_index("lat")
    half = lanes // 2

    def quantity(k):
        lane = k // 4 * half
        return jnp.concatenate(
            [gathered[:, y, k % 4, :][:, lane : lane + lines] for y in range(devices_y)], axis=1
        )

    first_source, last_source, first_ground, last_ground, edge, open_face, ocean = [quantity(k) for k in range(7)]
    ring = ring_setup(first_ground, last_ground, edge, open_face, ocean)
    first_ends, last_ends = ring_ends(first_source, last_source, *ring)
    first_ends, last_ends = own_row(first_ends, index_x), own_row(last_ends, index_x)
    current = jnp.concatenate(
        [
            payload[y, 0]
            + payload[y, 1] * columns(first_ends, y, height, levels, lanes)
            + payload[y, 2] * columns(last_ends, y, height, levels, lanes)
            for y in range(devices_y)
        ],
        axis=0,
    )
    open_face = jnp.concatenate([payload[y, 3] for y in range(devices_y)], axis=0)
    packed = jnp.concatenate([payload[y, 4] for y in range(devices_y)], axis=0)
    reciprocal = jnp.concatenate([packed[:, :half]] * levels, axis=1)
    ocean = jnp.concatenate([packed[:, half:]] * levels, axis=1)
    count = devices_y * height
    row = iota((count, lanes), 0)
    top = row == count - 1
    faces = jnp.where(top, 0.0, open_face * moved(ocean, -1, 0))
    factors, (ground, current, reach) = condense(
        moved(faces, 1, 0), faces, [jnp.ones_like(faces), current, top.astype(F32)], count, 0
    )
    inverse = 1.0 / ground
    current = current * inverse
    reach = reach * inverse
    again = relax(jnp.where(top, 0.0, current * reciprocal), factors, 0) * inverse

    def own_block(values):
        chosen = values[:height]
        for y in range(1, devices_y):
            chosen = jnp.where(index_y == y, values[y * height : (y + 1) * height], chosen)
        return chosen

    again, reach = own_block(again), own_block(reach)
    kept[0] = again
    kept[1] = reach
    rows = half_sums([keep[0] * again, keep[1] * again], levels)
    whole = jnp.concatenate(
        [
            keep[0] * reach,
            keep[1] * reach,
            jnp.concatenate([rows[:1], rows[1:2]], axis=1),
            current[count - 1 :],
            reciprocal[count - 1 :],
            jnp.zeros((5, lanes), F32),
        ],
        axis=0,
    )
    message[...] = jnp.broadcast_to(whole[None], message.shape)


def mirrored(values, pivot, width):
    count, lanes = values.shape
    devices = count // 2
    pivot_block, pivot_place = pivot // width, pivot % width
    source, target = iota((lanes, lanes), 0), iota((lanes, lanes), 1)
    reach = pivot_place - target % width
    same = source // width == target // width
    goal, origin = iota((count, count), 0), iota((count, count), 1)
    result = 0.0
    for extra in range(2):
        lane_pick = (same & (source % width == reach + extra * width)).astype(F32)
        turned = lax.dot(values, lane_pick, precision=EXACT, preferred_element_type=F32)
        wanted = (pivot_block - goal % devices - extra + 2 * devices) % devices
        block_pick = ((goal // devices == origin // devices) & (origin % devices == wanted)).astype(F32)
        result = result + lax.dot(block_pick, turned, precision=EXACT, preferred_element_type=F32)
    return result


def zonal_close(gathered, ring_rows, kept, factors_ref, keep, pairing, out):
    levels, height, width = out.shape
    lanes = levels * width
    lines = levels * height
    half = lanes // 2
    devices = gathered.shape[0]
    index_x, index_y = lax.axis_index("lon"), lax.axis_index("lat")
    mine = ring_rows[:, pl.ds(index_y, 1), :, :].reshape(devices, 4, lanes)
    ring = ring_setup(
        mine[:, 2, :lines],
        mine[:, 3, :lines],
        mine[:, 0, half : half + lines],
        mine[:, 1, half : half + lines],
        mine[:, 2, half : half + lines],
    )
    top, reciprocal = gathered[:, lines + 1, :], gathered[:, lines + 2, :]
    pivot = (pairing[0] + index_x * width) % (devices * width)
    across = mirrored(jnp.concatenate([top, reciprocal], axis=0), pivot, width)
    folded = 0.25 * (top + across[:devices]) * (reciprocal + across[devices:])
    tiled = jnp.concatenate([folded] * devices, axis=1)
    row, col = iota(tiled.shape, 0), iota(tiled.shape, 1)
    picks = jnp.concatenate(
        [jnp.where((col // lanes == row) & (col % lanes // width == k), tiled, 0.0) for k in range(levels)], axis=0
    )
    reach = jnp.concatenate([gathered[b, : 2 * height, :] for b in range(devices)], axis=1)
    change = lax.dot_general(
        picks, reach, (((1,), (1,)), ((), ())), precision=EXACT, preferred_element_type=F32
    )
    change = [change[k * devices : (k + 1) * devices] for k in range(levels)]
    first_source = gathered[:, lines, :][:, :lines] + jnp.concatenate([c[:, :height] for c in change], axis=1)
    last_source = gathered[:, lines, :][:, half : half + lines] + jnp.concatenate(
        [c[:, height:] for c in change], axis=1
    )
    first_ends, last_ends = ring_ends(first_source, last_source, *ring)
    current = kept[0] + kept[1] * own_row(folded, index_x)
    inner = keep[2] > 0.0
    direct = relax(jnp.where(inner, current, 0.0), load_factors(factors_ref), 1) * keep[2]

    def ends(values):
        own = own_row(values, index_x)
        return columns(jnp.concatenate([own, own], axis=1)[:, :lanes], 0, height, levels, lanes)

    result = keep[3] * (direct + keep[0] * ends(first_ends) + keep[1] * ends(last_ends))
    for k in range(levels):
        out[k] = result[:, k * width : (k + 1) * width]


def run(body, shapes, *operands, scalars=(), outside=(), scratch=(), limit=8 << 20):
    vmem = pl.BlockSpec(memory_space=pltpu.VMEM)
    smem = pl.BlockSpec(memory_space=pltpu.SMEM)
    hbm = pl.BlockSpec(memory_space=pltpu.HBM)
    return pl.pallas_call(
        body,
        out_shape=[jax.ShapeDtypeStruct(shape, F32) for shape in shapes],
        in_specs=[smem if k in scalars else hbm if k in outside else vmem for k in range(len(operands))],
        out_specs=[vmem] * len(shapes),
        scratch_shapes=scratch,
        compiler_params=pltpu.CompilerParams(vmem_limit_bytes=limit),
        name=body.__name__,
    )(*operands)


def local(field, gamma, kappa_zonal, kappa_merid, area, sea_mask, fold_pair):
    levels, height, width = field.shape
    lanes = levels * width
    devices_x, devices_y = lax.axis_size("lon"), lax.axis_size("lat")
    tile = (height, lanes)
    count = 2 * (width - 3).bit_length()
    operands = (field, gamma, kappa_zonal, kappa_merid, area, sea_mask)
    scratch = [pltpu.VMEM(x.shape, x.dtype) for x in operands] + [pltpu.SemaphoreType.DMA((len(operands),))]
    message, payload, factors, keep = run(
        block_local,
        [(devices_x * devices_y, 4, lanes), (5,) + tile, (count,) + tile, (4,) + tile],
        *operands,
        outside=range(len(operands)),
        scratch=scratch,
        limit=None,
    )
    ring_rows = lax.all_to_all(message, ("lon", "lat"), split_axis=0, concat_axis=0, tiled=True)
    ring_rows = ring_rows.reshape(devices_x, devices_y, 4, lanes)
    payload = lax.all_gather(payload, "lat", axis=0, tiled=False)
    kept, message = run(
        column_join, [(2,) + tile, (devices_x, 2 * height + 8, lanes)], ring_rows, payload, keep
    )
    gathered = lax.all_to_all(message, "lon", split_axis=0, concat_axis=0, tiled=True)
    (result,) = run(
        zonal_close, [(levels, height, width)], gathered, ring_rows, kept, factors, keep, fold_pair, scalars=(5,)
    )
    return result


def solution(mesh):
    blocks = P(None, "lat", "lon")
    return jax.shard_map(
        local,
        mesh=mesh,
        in_specs=(blocks, blocks, blocks, blocks, P("lat", "lon"), P("lat", "lon"), P("lon")),
        out_specs=blocks,
        check_vma=False,
    )
```

```python
import functools

import jax
import jax.numpy as jnp
from jax import lax
from jax.experimental import pallas as pl
from jax.experimental.pallas import tpu as pltpu
from jax.sharding import PartitionSpec as P


F32 = jnp.float32
EXACT = lax.Precision.HIGHEST


def moved(values, distance, axis):
    return pltpu.roll(values, distance % values.shape[axis], axis)


def iota(shape, axis):
    return lax.broadcasted_iota(jnp.int32, shape, axis)


def spread(values, up, down, stride, axis):
    return values + moved(up * values, stride, axis) + moved(down * values, -stride, axis)


def condense(left, right, totals, count, axis):
    factors = []
    stride = 1
    while stride < count:
        pull = 1.0 / (totals[0] + left + right)
        up, down = right * pull, left * pull
        link = left * up
        factors.append((up, down))
        totals = [spread(t, up, down, stride, axis) for t in totals]
        left, right = moved(link, stride, axis), moved(link, -stride, axis)
        stride *= 2
    return factors, totals


def relax(values, factors, axis):
    stride = 1
    for up, down in factors:
        values = spread(values, up, down, stride, axis)
        stride *= 2
    return values


def load_factors(ref):
    return [(ref[2 * k], ref[2 * k + 1]) for k in range(ref.shape[0] // 2)]


def store_factors(ref, factors):
    for k, (up, down) in enumerate(factors):
        ref[2 * k] = up
        ref[2 * k + 1] = down


def beside(ref):
    return jnp.concatenate([ref[k] for k in range(ref.shape[0])], axis=-1)


def chain(faces, place, length, axis):
    inner = (place >= 1) & (place <= length - 3)
    right = jnp.where(inner, faces, 0.0)
    left = moved(right, 1, axis)
    to_first = jnp.where(place == 1, moved(faces, 1, axis), 0.0)
    to_last = jnp.where(place == length - 2, faces, 0.0)
    return left, right, to_first, to_last


def half_sums(arrays, levels):
    wide = jnp.concatenate(arrays, axis=1)
    lanes = arrays[0].shape[1]
    width = lanes // levels
    shape = (8 * levels, wide.shape[1])
    row, col = iota(shape, 0), iota(shape, 1)
    pick = ((col // lanes == row % 8) & (col % lanes // width == row // 8)).astype(F32)
    sums = lax.dot_general(pick, wide, (((1,), (1,)), ((), ())), precision=EXACT, preferred_element_type=F32)
    return jnp.concatenate([sums[8 * k : 8 * k + 8] for k in range(levels)], axis=1)


def padded(rows, lanes):
    return jnp.concatenate([rows, jnp.zeros((rows.shape[0], lanes - rows.shape[1]), F32)], axis=1)


def fetch(sources, buffers, semaphores):
    copies = [
        pltpu.make_async_copy(source, buffer, semaphores.at[k])
        for k, (source, buffer) in enumerate(zip(sources, buffers))
    ]
    for copy in copies:
        copy.start()
    for copy in copies:
        copy.wait()


def block_local(*refs):
    sources, (message, payload, factors_out, keep, turn), buffers, semaphores = (
        refs[:7], refs[7:12], refs[12:19], refs[19]
    )
    fetch(sources, buffers, semaphores)
    field, gamma, kappa_zonal, kappa_merid, area, mask, pairing = buffers
    levels, height, width = field.shape
    lanes = levels * width
    ocean_one = mask[...].astype(F32)
    ocean = jnp.concatenate([ocean_one] * levels, axis=1)
    place = iota((height, lanes), 1) % width
    scaled = beside(gamma) * ocean
    source = scaled * beside(field)
    open_face = beside(kappa_zonal) * ocean
    faces = open_face * moved(ocean, -1, 1)
    left, right, to_first, to_last = chain(faces, place, width, 1)
    inner = (place >= 1) & (place <= width - 2)
    factors, (ground, first, last, direct) = condense(
        left,
        right,
        [1.0 + to_first + to_last, to_first, to_last, jnp.where(inner, source, 0.0)],
        width - 2,
        1,
    )
    inverse = jnp.where(inner, 1.0 / ground, 0.0)
    first = first * inverse
    last = last * inverse
    edge = to_first * last
    first = jnp.where(place == 0, 1.0, first)
    last = jnp.where(place == width - 1, 1.0, last)
    rows = half_sums(
        [
            first * source,
            last * source,
            first,
            last,
            edge,
            jnp.where(place == width - 1, open_face, 0.0),
            jnp.where(place == 0, ocean, 0.0),
        ],
        levels,
    )
    message[...] = jnp.broadcast_to(jnp.concatenate([rows[:4], rows[4:]], axis=1)[None], message.shape)
    payload[0] = direct * inverse
    payload[1] = first
    payload[2] = last
    payload[3] = beside(kappa_merid) * ocean
    payload[4] = jnp.concatenate([1.0 / area[...], ocean_one], axis=1)
    store_factors(factors_out, factors)
    keep[0] = first
    keep[1] = last
    keep[2] = inverse
    keep[3] = scaled
    turn[...] = jnp.full(turn.shape, pairing[0] + lax.axis_index("lon") * width, jnp.int32)


def ring_setup(first_ground, last_ground, edge, open_face, ocean):
    face = open_face * moved(ocean, -1, 0)
    last_pull = 1.0 / (last_ground + edge + face)
    edge_pull, face_pull = edge * last_pull, face * last_pull
    ground = first_ground + edge_pull * last_ground + moved(face_pull * last_ground, 1, 0)
    link = edge * face_pull
    factors, (ground,) = condense(moved(link, 1, 0), link, [ground], edge.shape[0], 0)
    return edge_pull, face_pull, last_pull, factors, 1.0 / ground


def ring_ends(first_source, last_source, edge_pull, face_pull, last_pull, factors, inverse):
    values = first_source + edge_pull * last_source + moved(face_pull * last_source, 1, 0)
    first = relax(values, factors, 0) * inverse
    last = last_pull * last_source + edge_pull * first + face_pull * moved(first, -1, 0)
    return first, last


def own_row(values, index):
    return jnp.sum(jnp.where(iota(values.shape, 0) == index, values, 0.0), axis=0, keepdims=True)


def columns(own, block, height, levels, lanes):
    width = lanes // levels
    row, col = iota((height, lanes), 0), iota((height, lanes), 1)
    result = None
    for k in range(levels):
        base = (block * levels + k) * height
        group = own[:, base // lanes * lanes : base // lanes * lanes + lanes]
        column = jnp.sum(jnp.where(col == row + base % lanes, group, 0.0), axis=1, keepdims=True)
        result = jnp.broadcast_to(column, (height, lanes)) if k == 0 else jnp.where(col >= k * width, column, result)
    return result


def column_join(gathered, payload, keep, kept, message):
    levels = 2
    devices_y, _, height, lanes = payload.shape
    lines = levels * height
    index_x, index_y = lax.axis_index("lon"), lax.axis_index("lat")
    half = lanes // 2

    def quantity(k):
        lane = k // 4 * half
        return jnp.concatenate(
            [gathered[:, y, k % 4, :][:, lane : lane + lines] for y in range(devices_y)], axis=1
        )

    first_source, last_source, first_ground, last_ground, edge, open_face, ocean = [quantity(k) for k in range(7)]
    ring = ring_setup(first_ground, last_ground, edge, open_face, ocean)
    first_ends, last_ends = ring_ends(first_source, last_source, *ring)
    first_ends, last_ends = own_row(first_ends, index_x), own_row(last_ends, index_x)
    current = jnp.concatenate(
        [
            payload[y, 0]
            + payload[y, 1] * columns(first_ends, y, height, levels, lanes)
            + payload[y, 2] * columns(last_ends, y, height, levels, lanes)
            for y in range(devices_y)
        ],
        axis=0,
    )
    open_face = jnp.concatenate([payload[y, 3] for y in range(devices_y)], axis=0)
    packed = jnp.concatenate([payload[y, 4] for y in range(devices_y)], axis=0)
    reciprocal = jnp.concatenate([packed[:, :half]] * levels, axis=1)
    ocean = jnp.concatenate([packed[:, half:]] * levels, axis=1)
    count = devices_y * height
    row = iota((count, lanes), 0)
    top = row == count - 1
    faces = jnp.where(top, 0.0, open_face * moved(ocean, -1, 0))
    factors, (ground, current, reach) = condense(
        moved(faces, 1, 0), faces, [jnp.ones_like(faces), current, top.astype(F32)], count, 0
    )
    inverse = 1.0 / ground
    current = current * inverse
    reach = reach * inverse
    again = relax(jnp.where(top, 0.0, current * reciprocal), factors, 0) * inverse

    def own_block(values):
        chosen = values[:height]
        for y in range(1, devices_y):
            chosen = jnp.where(index_y == y, values[y * height : (y + 1) * height], chosen)
        return chosen

    again, reach = own_block(again), own_block(reach)
    kept[0] = again
    kept[1] = reach
    rows = half_sums([keep[0] * again, keep[1] * again], levels)
    whole = jnp.concatenate(
        [
            keep[0] * reach,
            keep[1] * reach,
            jnp.concatenate([rows[:1], rows[1:2]], axis=1),
            current[count - 1 :],
            reciprocal[count - 1 :],
            jnp.zeros((5, lanes), F32),
        ],
        axis=0,
    )
    message[...] = jnp.broadcast_to(whole[None], message.shape)


def mirrored(rows, pivot, width):
    devices, lanes = rows[0].shape
    block, lane = iota((devices, lanes), 0), iota((devices, lanes), 1)
    place = lane % width
    pivot_block, pivot_place = pivot // width % devices, pivot % width
    reach = lane - place + (pivot_place - place + width) % width
    wanted = (pivot_block - block - (place > pivot_place).astype(jnp.int32) + 2 * devices) % devices
    results = []
    for values in rows:
        turned = jnp.take_along_axis(values, reach, axis=1)
        result = turned
        for b in range(devices):
            result = jnp.where(wanted == b, turned[b : b + 1], result)
        results.append(result)
    return results


def zonal_close(gathered, ring_rows, kept, factors_ref, keep, turn, out):
    levels, height, width = out.shape
    lanes = levels * width
    lines = levels * height
    half = lanes // 2
    devices = gathered.shape[0]
    index_x, index_y = lax.axis_index("lon"), lax.axis_index("lat")
    mine = ring_rows[:, pl.ds(index_y, 1), :, :].reshape(devices, 4, lanes)
    ring = ring_setup(
        mine[:, 2, :lines],
        mine[:, 3, :lines],
        mine[:, 0, half : half + lines],
        mine[:, 1, half : half + lines],
        mine[:, 2, half : half + lines],
    )
    top, reciprocal = gathered[:, lines + 1, :], gathered[:, lines + 2, :]
    top_across, reciprocal_across = mirrored([top, reciprocal], turn[:devices], width)
    folded = 0.25 * (top + top_across) * (reciprocal + reciprocal_across)
    tiled = jnp.concatenate([folded] * devices, axis=1)
    row, col = iota(tiled.shape, 0), iota(tiled.shape, 1)
    picks = jnp.concatenate(
        [jnp.where((col // lanes == row) & (col % lanes // width == k), tiled, 0.0) for k in range(levels)], axis=0
    )
    reach = jnp.concatenate([gathered[b, : 2 * height, :] for b in range(devices)], axis=1)
    change = lax.dot_general(
        picks, reach, (((1,), (1,)), ((), ())), precision=EXACT, preferred_element_type=F32
    )
    change = [change[k * devices : (k + 1) * devices] for k in range(levels)]
    first_source = gathered[:, lines, :][:, :lines] + jnp.concatenate([c[:, :height] for c in change], axis=1)
    last_source = gathered[:, lines, :][:, half : half + lines] + jnp.concatenate(
        [c[:, height:] for c in change], axis=1
    )
    first_ends, last_ends = ring_ends(first_source, last_source, *ring)
    current = kept[0] + kept[1] * own_row(folded, index_x)
    inner = keep[2] > 0.0
    direct = relax(jnp.where(inner, current, 0.0), load_factors(factors_ref), 1) * keep[2]

    def ends(values):
        own = own_row(values, index_x)
        return columns(jnp.concatenate([own, own], axis=1)[:, :lanes], 0, height, levels, lanes)

    result = keep[3] * (direct + keep[0] * ends(first_ends) + keep[1] * ends(last_ends))
    for k in range(levels):
        out[k] = result[:, k * width : (k + 1) * width]


def run(body, shapes, *operands, outside=False, scratch=()):
    vmem = pl.BlockSpec(memory_space=pltpu.VMEM)
    hbm = pl.BlockSpec(memory_space=pltpu.HBM)
    if outside:
        operands = [pltpu.with_memory_space_constraint(x, pltpu.HBM) for x in operands]
    return pl.pallas_call(
        body,
        out_shape=shapes,
        in_specs=[hbm if outside else vmem] * len(operands),
        out_specs=[vmem] * len(shapes),
        scratch_shapes=scratch,
        compiler_params=pltpu.CompilerParams(vmem_limit_bytes=8 << 20),
        name=body.__name__,
    )(*operands)


def array(*shape, dtype=F32):
    return jax.ShapeDtypeStruct(shape, dtype)


def local(field, gamma, kappa_zonal, kappa_merid, area, sea_mask, fold_pair):
    levels, height, width = field.shape
    lanes = levels * width
    devices_x, devices_y = lax.axis_size("lon"), lax.axis_size("lat")
    count = 2 * (width - 3).bit_length()
    operands = (field, gamma, kappa_zonal, kappa_merid, area, sea_mask, fold_pair)
    scratch = [pltpu.VMEM(x.shape, x.dtype) for x in operands[:-1]]
    scratch += [pltpu.SMEM(fold_pair.shape, fold_pair.dtype), pltpu.SemaphoreType.DMA((len(operands),))]
    message, payload, factors, keep, turn = run(
        block_local,
        [
            array(devices_x * devices_y, 4, lanes),
            array(5, height, lanes),
            array(count, height, lanes),
            array(4, height, lanes),
            array(devices_x, lanes, dtype=jnp.int32),
        ],
        *operands,
        outside=True,
        scratch=scratch,
    )
    ring_rows = lax.all_to_all(message, ("lon", "lat"), split_axis=0, concat_axis=0, tiled=True)
    ring_rows = ring_rows.reshape(devices_x, devices_y, 4, lanes)
    payload = lax.all_gather(payload, "lat", axis=0, tiled=False)
    kept, message = run(
        column_join,
        [array(2, height, lanes), array(devices_x, 2 * height + 8, lanes)],
        ring_rows, payload, keep,
    )
    gathered = lax.all_to_all(message, "lon", split_axis=0, concat_axis=0, tiled=True)
    (result,) = run(
        zonal_close, [array(levels, height, width)], gathered, ring_rows, kept, factors, keep, turn
    )
    return result


def solution(mesh):
    blocks = P(None, "lat", "lon")
    return jax.shard_map(
        local,
        mesh=mesh,
        in_specs=(blocks, blocks, blocks, blocks, P("lat", "lon"), P("lat", "lon"), P("lon")),
        out_specs=blocks,
        check_vma=False,
    )
```

```python
import functools

import jax
import jax.numpy as jnp
from jax import lax
from jax.experimental import pallas as pl
from jax.experimental.pallas import tpu as pltpu
from jax.sharding import PartitionSpec as P


F32 = jnp.float32
EXACT = lax.Precision.HIGHEST


def moved(values, distance, axis):
    return pltpu.roll(values, distance % values.shape[axis], axis)


def iota(shape, axis):
    return lax.broadcasted_iota(jnp.int32, shape, axis)


def spread(values, up, down, stride, axis):
    return values + moved(up * values, stride, axis) + moved(down * values, -stride, axis)


def condense(left, right, totals, count, axis):
    factors = []
    stride = 1
    while stride < count:
        pull = 1.0 / (totals[0] + left + right)
        up, down = right * pull, left * pull
        link = left * up
        factors.append((up, down))
        totals = [spread(t, up, down, stride, axis) for t in totals]
        left, right = moved(link, stride, axis), moved(link, -stride, axis)
        stride *= 2
    return factors, totals


def relax(values, factors, axis):
    stride = 1
    for up, down in factors:
        values = spread(values, up, down, stride, axis)
        stride *= 2
    return values


def load_factors(ref):
    return [(ref[2 * k], ref[2 * k + 1]) for k in range(ref.shape[0] // 2)]


def store_factors(ref, factors):
    for k, (up, down) in enumerate(factors):
        ref[2 * k] = up
        ref[2 * k + 1] = down


def beside(ref):
    return jnp.concatenate([ref[k] for k in range(ref.shape[0])], axis=-1)


def chain(faces, place, length, axis):
    inner = (place >= 1) & (place <= length - 3)
    right = jnp.where(inner, faces, 0.0)
    left = moved(right, 1, axis)
    to_first = jnp.where(place == 1, moved(faces, 1, axis), 0.0)
    to_last = jnp.where(place == length - 2, faces, 0.0)
    return left, right, to_first, to_last


def half_sums(arrays, levels):
    wide = jnp.concatenate(arrays, axis=1)
    lanes = arrays[0].shape[1]
    width = lanes // levels
    shape = (8 * levels, wide.shape[1])
    row, col = iota(shape, 0), iota(shape, 1)
    pick = ((col // lanes == row % 8) & (col % lanes // width == row // 8)).astype(F32)
    sums = lax.dot_general(pick, wide, (((1,), (1,)), ((), ())), precision=EXACT, preferred_element_type=F32)
    return jnp.concatenate([sums[8 * k : 8 * k + 8] for k in range(levels)], axis=1)


def padded(rows, lanes):
    return jnp.concatenate([rows, jnp.zeros((rows.shape[0], lanes - rows.shape[1]), F32)], axis=1)


def fetch(sources, buffers, semaphores):
    copies = [
        pltpu.make_async_copy(source, buffer, semaphores.at[k])
        for k, (source, buffer) in enumerate(zip(sources, buffers))
    ]
    for copy in copies:
        copy.start()
    for copy in copies:
        copy.wait()


def zonal_block(field, gamma, kappa_zonal, ocean):
    levels, height, width = field.shape
    place = iota((height, levels * width), 1) % width
    scaled = beside(gamma) * ocean
    source = scaled * beside(field)
    open_face = beside(kappa_zonal) * ocean
    faces = open_face * moved(ocean, -1, 1)
    left, right, to_first, to_last = chain(faces, place, width, 1)
    inner = (place >= 1) & (place <= width - 2)
    factors, (ground, first, last, direct) = condense(
        left,
        right,
        [1.0 + to_first + to_last, to_first, to_last, jnp.where(inner, source, 0.0)],
        width - 2,
        1,
    )
    inverse = jnp.where(inner, 1.0 / ground, 0.0)
    first = first * inverse
    last = last * inverse
    edge = to_first * last
    first = jnp.where(place == 0, 1.0, first)
    last = jnp.where(place == width - 1, 1.0, last)
    outward = jnp.where(place == width - 1, open_face, 0.0)
    terms = [first * source, first, edge, last * source, last, outward]
    return factors, scaled, inverse, direct * inverse, first, last, terms


def unpack(refs):
    sources, outputs, buffers, semaphores = refs[:7], refs[7:12], refs[12:19], refs[19]
    fetch(sources, buffers, semaphores)
    return outputs, buffers


def fold_sum(pairing, width):
    return pairing[0] + lax.axis_index("lon") * width


def block_local(*refs):
    (message, payload, factors_out, keep, turn), buffers = unpack(refs)
    field, gamma, kappa_zonal, kappa_merid, area, mask, pairing = buffers
    levels, height, width = field.shape
    ocean_one = mask[...].astype(F32)
    ocean = jnp.concatenate([ocean_one] * levels, axis=1)
    factors, scaled, inverse, direct, first, last, terms = zonal_block(field, gamma, kappa_zonal, ocean)
    place = iota(first.shape, 1) % width
    order = [terms[0], terms[3], terms[1], terms[4], terms[2], terms[5]]
    rows = half_sums(order + [jnp.where(place == 0, ocean, 0.0)], levels)
    message[...] = jnp.broadcast_to(jnp.concatenate([rows[:4], rows[4:]], axis=1)[None], message.shape)
    payload[0] = direct
    payload[1] = first
    payload[2] = last
    payload[3] = beside(kappa_merid) * ocean
    payload[4] = jnp.concatenate([1.0 / area[...], ocean_one], axis=1)
    store_factors(factors_out, factors)
    keep[0] = first
    keep[1] = last
    keep[2] = inverse
    keep[3] = scaled
    turn[...] = jnp.full(turn.shape, fold_sum(pairing, width), jnp.int32)


def ring_setup(first_ground, last_ground, edge, open_face, ocean):
    face = open_face * moved(ocean, -1, 0)
    last_pull = 1.0 / (last_ground + edge + face)
    edge_pull, face_pull = edge * last_pull, face * last_pull
    ground = first_ground + edge_pull * last_ground + moved(face_pull * last_ground, 1, 0)
    link = edge * face_pull
    factors, (ground,) = condense(moved(link, 1, 0), link, [ground], edge.shape[0], 0)
    return edge_pull, face_pull, last_pull, factors, 1.0 / ground


def ring_ends(first_source, last_source, edge_pull, face_pull, last_pull, factors, inverse):
    values = first_source + edge_pull * last_source + moved(face_pull * last_source, 1, 0)
    first = relax(values, factors, 0) * inverse
    last = last_pull * last_source + edge_pull * first + face_pull * moved(first, -1, 0)
    return first, last


def own_row(values, index):
    return jnp.sum(jnp.where(iota(values.shape, 0) == index, values, 0.0), axis=0, keepdims=True)


def columns(own, block, height, levels, lanes):
    width = lanes // levels
    row, col = iota((height, lanes), 0), iota((height, lanes), 1)
    result = None
    for k in range(levels):
        base = (block * levels + k) * height
        group = own[:, base // lanes * lanes : base // lanes * lanes + lanes]
        column = jnp.sum(jnp.where(col == row + base % lanes, group, 0.0), axis=1, keepdims=True)
        result = jnp.broadcast_to(column, (height, lanes)) if k == 0 else jnp.where(col >= k * width, column, result)
    return result


def column_join(gathered, payload, keep, kept, message):
    levels = 2
    devices_y, _, height, lanes = payload.shape
    lines = levels * height
    index_x, index_y = lax.axis_index("lon"), lax.axis_index("lat")
    half = lanes // 2

    def quantity(k):
        lane = k // 4 * half
        return jnp.concatenate(
            [gathered[:, y, k % 4, :][:, lane : lane + lines] for y in range(devices_y)], axis=1
        )

    first_source, last_source, first_ground, last_ground, edge, open_face, ocean = [quantity(k) for k in range(7)]
    ring = ring_setup(first_ground, last_ground, edge, open_face, ocean)
    first_ends, last_ends = ring_ends(first_source, last_source, *ring)
    first_ends, last_ends = own_row(first_ends, index_x), own_row(last_ends, index_x)
    current = jnp.concatenate(
        [
            payload[y, 0]
            + payload[y, 1] * columns(first_ends, y, height, levels, lanes)
            + payload[y, 2] * columns(last_ends, y, height, levels, lanes)
            for y in range(devices_y)
        ],
        axis=0,
    )
    open_face = jnp.concatenate([payload[y, 3] for y in range(devices_y)], axis=0)
    packed = jnp.concatenate([payload[y, 4] for y in range(devices_y)], axis=0)
    reciprocal = jnp.concatenate([packed[:, :half]] * levels, axis=1)
    ocean = jnp.concatenate([packed[:, half:]] * levels, axis=1)
    count = devices_y * height
    row = iota((count, lanes), 0)
    top = row == count - 1
    faces = jnp.where(top, 0.0, open_face * moved(ocean, -1, 0))
    factors, (ground, current, reach) = condense(
        moved(faces, 1, 0), faces, [jnp.ones_like(faces), current, top.astype(F32)], count, 0
    )
    inverse = 1.0 / ground
    current = current * inverse
    reach = reach * inverse
    again = relax(jnp.where(top, 0.0, current * reciprocal), factors, 0) * inverse

    def own_block(values):
        chosen = values[:height]
        for y in range(1, devices_y):
            chosen = jnp.where(index_y == y, values[y * height : (y + 1) * height], chosen)
        return chosen

    again, reach = own_block(again), own_block(reach)
    kept[0] = again
    kept[1] = reach
    rows = half_sums([keep[0] * again, keep[1] * again], levels)
    whole = jnp.concatenate(
        [
            keep[0] * reach,
            keep[1] * reach,
            jnp.concatenate([rows[:1], rows[1:2]], axis=1),
            current[count - 1 :],
            reciprocal[count - 1 :],
            jnp.zeros((5, lanes), F32),
        ],
        axis=0,
    )
    message[...] = jnp.broadcast_to(whole[None], message.shape)


def mirrored(rows, pivot, width):
    devices, lanes = rows[0].shape
    block, lane = iota((devices, lanes), 0), iota((devices, lanes), 1)
    place = lane % width
    pivot_block, pivot_place = pivot // width % devices, pivot % width
    reach = lane - place + (pivot_place - place + width) % width
    wanted = (pivot_block - block - (place > pivot_place).astype(jnp.int32) + 2 * devices) % devices
    results = []
    for values in rows:
        turned = jnp.take_along_axis(values, reach, axis=1)
        result = turned
        for b in range(devices):
            result = jnp.where(wanted == b, turned[b : b + 1], result)
        results.append(result)
    return results


def zonal_close(gathered, ring_rows, kept, factors_ref, keep, turn, out):
    levels, height, width = out.shape
    lanes = levels * width
    lines = levels * height
    half = lanes // 2
    devices = gathered.shape[0]
    index_x, index_y = lax.axis_index("lon"), lax.axis_index("lat")
    mine = ring_rows[:, pl.ds(index_y, 1), :, :].reshape(devices, 4, lanes)
    ring = ring_setup(
        mine[:, 2, :lines],
        mine[:, 3, :lines],
        mine[:, 0, half : half + lines],
        mine[:, 1, half : half + lines],
        mine[:, 2, half : half + lines],
    )
    top, reciprocal = gathered[:, lines + 1, :], gathered[:, lines + 2, :]
    top_across, reciprocal_across = mirrored([top, reciprocal], turn[:devices], width)
    folded = 0.25 * (top + top_across) * (reciprocal + reciprocal_across)
    tiled = jnp.concatenate([folded] * devices, axis=1)
    row, col = iota(tiled.shape, 0), iota(tiled.shape, 1)
    picks = jnp.concatenate(
        [jnp.where((col // lanes == row) & (col % lanes // width == k), tiled, 0.0) for k in range(levels)], axis=0
    )
    reach = jnp.concatenate([gathered[b, : 2 * height, :] for b in range(devices)], axis=1)
    change = lax.dot_general(
        picks, reach, (((1,), (1,)), ((), ())), precision=EXACT, preferred_element_type=F32
    )
    change = [change[k * devices : (k + 1) * devices] for k in range(levels)]
    first_source = gathered[:, lines, :][:, :lines] + jnp.concatenate([c[:, :height] for c in change], axis=1)
    last_source = gathered[:, lines, :][:, half : half + lines] + jnp.concatenate(
        [c[:, height:] for c in change], axis=1
    )
    first_ends, last_ends = ring_ends(first_source, last_source, *ring)
    current = kept[0] + kept[1] * own_row(folded, index_x)
    inner = keep[2] > 0.0
    direct = relax(jnp.where(inner, current, 0.0), load_factors(factors_ref), 1) * keep[2]

    result = keep[3] * (
        direct
        + keep[0] * spread_ends(first_ends, index_x, height, levels, lanes)
        + keep[1] * spread_ends(last_ends, index_x, height, levels, lanes)
    )
    for k in range(levels):
        out[k] = result[:, k * width : (k + 1) * width]


def run(body, shapes, *operands, outside=False, scratch=()):
    vmem = pl.BlockSpec(memory_space=pltpu.VMEM)
    hbm = pl.BlockSpec(memory_space=pltpu.HBM)
    if outside:
        operands = [pltpu.with_memory_space_constraint(x, pltpu.HBM) for x in operands]
    return pl.pallas_call(
        body,
        out_shape=shapes,
        in_specs=[hbm if outside else vmem] * len(operands),
        out_specs=[vmem] * len(shapes),
        scratch_shapes=scratch,
        compiler_params=pltpu.CompilerParams(vmem_limit_bytes=8 << 20),
        name=body.__name__,
    )(*operands)


def array(*shape, dtype=F32):
    return jax.ShapeDtypeStruct(shape, dtype)


def column_order(place, width):
    return jnp.where(place < width // 2, place, width + width // 2 - 1 - place)


def block_send(*refs):
    (message, factors_out, keep, turn), buffers = unpack_four(refs)
    field, gamma, kappa_zonal, kappa_merid, area, mask, pairing = buffers
    levels, height, width = field.shape
    lanes = levels * width
    half = width // 2
    ocean_one = mask[...].astype(F32)
    ocean = jnp.concatenate([ocean_one] * levels, axis=1)
    factors, scaled, inverse, direct, first, last, terms = zonal_block(field, gamma, kappa_zonal, ocean)
    devices = message.shape[0]
    centre = (fold_sum(pairing, width) % (lax.axis_size("lon") * width) + 1) // 2
    row = iota((height, lanes), 0)
    merid = beside(kappa_merid) * jnp.where(row == height - 1, ocean, ocean * moved(ocean, -1, 0))
    lane = iota((height, lanes), 1)
    reach = lane // width * width + (column_order(lane % width, width) + centre) % width

    def ordered(values):
        return jnp.take_along_axis(values, reach, axis=1)

    pieces = jnp.concatenate([ordered(x) for x in (direct, first, last, merid)], axis=0).T
    for k, start in enumerate((0, width, half, width + half)):
        message[:, k, :] = pieces[start : start + devices]
    packed = ordered(jnp.concatenate([1.0 / area[...], ocean_one], axis=1))

    def tile(distance):
        return jnp.broadcast_to(moved(packed, distance, 1)[:1], (8, lanes))

    extra = jnp.concatenate(
        [
            packed,
            jnp.broadcast_to(ocean_one[:, :1], (height, lanes)),
            tile(-width - half),
            moved(packed, -half, 1),
            jnp.zeros((lanes - 3 * height - 16, lanes), F32),
            tile(-width),
        ],
        axis=0,
    ).T
    message[:, 4, :] = extra[:devices]
    rows = half_sums(terms, levels)
    for k in range(3):
        both = jnp.concatenate([rows[k : k + 1], rows[k + 3 : k + 4]], axis=1)
        message[:, 5 + k, :] = jnp.broadcast_to(both, (devices, lanes))
    store_factors(factors_out, factors)
    keep[0] = first
    keep[1] = last
    keep[2] = inverse
    keep[3] = scaled
    turn[...] = jnp.full(turn.shape, centre, jnp.int32)


def unpack_four(refs):
    sources, outputs, buffers, semaphores = refs[:7], refs[7:11], refs[11:18], refs[18]
    fetch(sources, buffers, semaphores)
    return outputs, buffers


def column_solve(gathered, turn, message, hold):
    devices_x, devices_y, tall, lanes = gathered.shape
    height = lanes // devices_y
    width = devices_x * devices_y * 2
    levels = 2
    shape = (devices_x * tall, lanes)
    small = iota((devices_x, lanes), 1) // height
    lane = iota(shape, 1)
    line = iota(shape, 0) % tall
    lats = range(devices_y)

    def merged(parts, where, target):
        result = None
        for k, values in enumerate(parts):
            turned = moved(values, (k - where[k]) * height, 1)
            result = turned if k == 0 else jnp.where(target == k, turned, result)
        return result

    def ring_term(r, f):
        parts = [gathered[:, y, r, :] for y in lats]
        return jnp.concatenate(
            [merged(parts, [f * levels + h] * devices_y, small) for h in range(levels)], axis=1
        )

    first_source, last_source = ring_term(5, 0), ring_term(5, 1)
    first_ground, last_ground = ring_term(6, 0), ring_term(6, 1)
    edge, open_face = ring_term(7, 0), ring_term(7, 1)
    ocean = merged([gathered[:, y, 4, :] for y in lats], [1] * devices_y, small)
    ring = ring_setup(first_ground, last_ground, edge, open_face, jnp.concatenate([ocean] * levels, axis=1))
    first_ends, last_ends = ring_ends(first_source, last_source, *ring)

    def at_columns(ends):
        even = iota((tall, lanes), 0) % levels == 0
        return jnp.concatenate(
            [jnp.where(even, ends[b : b + 1, :lanes], ends[b : b + 1, lanes:]) for b in range(devices_x)], axis=0
        )

    tiles = [gathered[:, y, :, :].reshape(shape) for y in lats]
    direct, first, last, faces = [merged(tiles, [k] * devices_y, lane // height) for k in range(4)]
    used = line < 4
    current = jnp.where(used, direct + first * at_columns(first_ends) + last * at_columns(last_ends), 0.0)
    reciprocal, beyond = jnp.ones(shape, F32), jnp.zeros(shape, F32)
    for y in lats:
        extra = jnp.broadcast_to(gathered[:, y, 4:5, :], (devices_x, tall, lanes)).reshape(shape)
        turned = jnp.where(
            line < 2, moved(extra, y * height, 1), moved(extra, (y - 2) * height - 8, 1)
        )
        reciprocal = jnp.where(lane // height == y, turned, reciprocal)
        if y > 0:
            beyond = jnp.where(lane == y * height - 1, turned, beyond)
    faces = jnp.where(used, jnp.where(lane % height == height - 1, faces * beyond, faces), 0.0)
    factors, (ground, current) = condense(
        moved(faces, 1, 1), faces, [jnp.ones(shape, F32), current], lanes, 1
    )
    inverse = 1.0 / ground
    current = current * inverse

    index = lax.axis_index("lon") * devices_y + lax.axis_index("lat")
    centre = turn[...]
    block, place = centre // width, centre % width
    offset = devices_x - 1 + 2 * block
    offset = offset + (index + place >= width).astype(jnp.int32) + (place - 1 - index >= 0).astype(jnp.int32)

    def across(values):
        parts = []
        for b in range(devices_x):
            wanted = (offset - b + devices_x) % devices_x
            part = values[:tall]
            for k in range(1, devices_x):
                part = jnp.where(wanted == k, values[k * tall : (k + 1) * tall], part)
            parts.append(part)
        other = jnp.concatenate(parts, axis=0)
        return jnp.where(line < 2, moved(other, -2, 0), moved(other, 2, 0))

    folded = 0.25 * (current + across(current)) * (reciprocal + across(reciprocal))
    current = jnp.where(lane == lanes - 1, folded, current * reciprocal)
    current = relax(current, factors, 1) * inverse

    first, last = first * current, last * current
    first, last = first + moved(first, -2, 0), last + moved(last, -2, 0)
    hold[0] = jnp.where(line < 2, first, moved(last, 2, 0)).reshape(hold.shape[1:])
    hold[1] = current.reshape(hold.shape[1:])
    row = iota((devices_x, lanes), 0)
    for y in lats:
        ends, own = [
            merged([hold[k, :, r, :] for r in range(4)], [y] * 4, small) for k in range(2)
        ]
        for b in range(devices_x):
            message[b, y] = jnp.where(row == b, own, ends)


def block_close(gathered, ring_rows, factors_ref, keep, turn, out):
    levels, height, width = out.shape
    lanes = levels * width
    lines = levels * height
    half = width // 2
    devices = gathered.shape[0]
    index_x, index_y = lax.axis_index("lon"), lax.axis_index("lat")
    mine = ring_rows[:, pl.ds(index_y, 1), :, :].reshape(ring_rows.shape[0], ring_rows.shape[2], lanes)
    ocean = mine[:, 4, height : 2 * height]
    ring = ring_setup(
        mine[:, 6, :lines],
        mine[:, 6, lines:],
        mine[:, 7, :lines],
        mine[:, 7, lines:],
        jnp.concatenate([ocean] * levels, axis=1),
    )
    own = gathered[:, pl.ds(index_x, 1), :].reshape(devices, lanes)
    turned = jnp.concatenate([moved(own, -k * height, 1) for k in (0, 2, 1, 3)], axis=0).T[:height]
    lane = iota((height, lanes), 1)
    centre = jnp.broadcast_to(turn[:1], (height, lanes))
    reach = lane // width * width + column_order((lane - centre + 8 * width) % width, width)
    current = jnp.take_along_axis(turned, reach, axis=1)
    sums = jnp.sum(gathered[...], axis=0)
    rows = half_sums([keep[0] * current, keep[1] * current], levels)
    chosen = iota((sums.shape[0], lines), 0) == index_x
    first_source = jnp.where(chosen, rows[:1], sums[:, :lines])
    last_source = jnp.where(chosen, rows[1:2], sums[:, lines:])
    first_ends, last_ends = ring_ends(first_source, last_source, *ring)
    inner = keep[2] > 0.0
    direct = relax(jnp.where(inner, current, 0.0), load_factors(factors_ref), 1) * keep[2]
    result = keep[3] * (
        direct
        + keep[0] * spread_ends(first_ends, index_x, height, levels, lanes)
        + keep[1] * spread_ends(last_ends, index_x, height, levels, lanes)
    )
    for k in range(levels):
        out[k] = result[:, k * width : (k + 1) * width]


def spread_ends(values, index, height, levels, lanes):
    own = own_row(values, index)
    return columns(jnp.concatenate([own, own], axis=1)[:, :lanes], 0, height, levels, lanes)


def local_by_columns(operands, scratch, count):
    levels, height, width = operands[0].shape
    lanes = levels * width
    devices_x, devices_y = lax.axis_size("lon"), lax.axis_size("lat")
    devices = devices_x * devices_y
    message, factors, keep, turn = run(
        block_send,
        [
            array(devices, 8, lanes),
            array(count, height, lanes),
            array(4, height, lanes),
            array(8, lanes, dtype=jnp.int32),
        ],
        *operands,
        outside=True,
        scratch=scratch,
    )
    both = ("lon", "lat")
    ring_rows = lax.all_to_all(message, both, split_axis=0, concat_axis=0, tiled=True)
    ring_rows = ring_rows.reshape(devices_x, devices_y, 8, lanes)
    (message,) = run(
        column_solve,
        [array(devices_x, devices_y, devices_x, lanes)],
        ring_rows,
        turn,
        scratch=[pltpu.VMEM((2, devices_x, 8, lanes), F32)],
    )
    message = message.reshape(devices, devices_x, lanes)
    gathered = lax.all_to_all(message, both, split_axis=0, concat_axis=0, tiled=True)
    (result,) = run(
        block_close, [array(levels, height, width)], gathered, ring_rows, factors, keep, turn
    )
    return result


def local(field, gamma, kappa_zonal, kappa_merid, area, sea_mask, fold_pair):
    levels, height, width = field.shape
    lanes = levels * width
    devices_x, devices_y = lax.axis_size("lon"), lax.axis_size("lat")
    count = 2 * (width - 3).bit_length()
    operands = (field, gamma, kappa_zonal, kappa_merid, area, sea_mask, fold_pair)
    scratch = [pltpu.VMEM(x.shape, x.dtype) for x in operands[:-1]]
    scratch += [pltpu.SMEM(fold_pair.shape, fold_pair.dtype), pltpu.SemaphoreType.DMA((len(operands),))]
    if width == 2 * devices_x * devices_y and levels == 2 and devices_y * height == lanes == 4 * height:
        return local_by_columns(operands, scratch, count)
    message, payload, factors, keep, turn = run(
        block_local,
        [
            array(devices_x * devices_y, 4, lanes),
            array(5, height, lanes),
            array(count, height, lanes),
            array(4, height, lanes),
            array(devices_x, lanes, dtype=jnp.int32),
        ],
        *operands,
        outside=True,
        scratch=scratch,
    )
    ring_rows = lax.all_to_all(message, ("lon", "lat"), split_axis=0, concat_axis=0, tiled=True)
    ring_rows = ring_rows.reshape(devices_x, devices_y, 4, lanes)
    payload = lax.all_gather(payload, "lat", axis=0, tiled=False)
    kept, message = run(
        column_join,
        [array(2, height, lanes), array(devices_x, 2 * height + 8, lanes)],
        ring_rows, payload, keep,
    )
    gathered = lax.all_to_all(message, "lon", split_axis=0, concat_axis=0, tiled=True)
    (result,) = run(
        zonal_close, [array(levels, height, width)], gathered, ring_rows, kept, factors, keep, turn
    )
    return result


def solution(mesh):
    blocks = P(None, "lat", "lon")
    return jax.shard_map(
        local,
        mesh=mesh,
        in_specs=(blocks, blocks, blocks, blocks, P("lat", "lon"), P("lat", "lon"), P("lon")),
        out_specs=blocks,
        check_vma=False,
    )
```

```python
import functools

import jax
import jax.numpy as jnp
from jax import lax
from jax.experimental import pallas as pl
from jax.experimental.pallas import tpu as pltpu
from jax.sharding import PartitionSpec as P


F32 = jnp.float32
EXACT = lax.Precision.HIGHEST


def moved(values, distance, axis):
    distance %= values.shape[axis]
    return pltpu.roll(values, distance, axis) if distance else values


def iota(shape, axis):
    return lax.broadcasted_iota(jnp.int32, shape, axis)


def spread(values, up, down, stride, axis):
    return values + moved(up * values, stride, axis) + moved(down * values, -stride, axis)


def condense(left, right, totals, count, axis):
    factors = []
    stride = 1
    while stride < count:
        pull = 1.0 / (totals[0] + left + right)
        up, down = right * pull, left * pull
        link = left * up
        factors.append((up, down))
        totals = [spread(t, up, down, stride, axis) for t in totals]
        left, right = moved(link, stride, axis), moved(link, -stride, axis)
        stride *= 2
    return factors, totals


def relax(values, factors, axis):
    stride = 1
    for up, down in factors:
        values = spread(values, up, down, stride, axis)
        stride *= 2
    return values


def load_factors(ref):
    return [(ref[2 * k], ref[2 * k + 1]) for k in range(ref.shape[0] // 2)]


def store_factors(ref, factors):
    for k, (up, down) in enumerate(factors):
        ref[2 * k] = up
        ref[2 * k + 1] = down


def beside(ref):
    return jnp.concatenate([ref[k] for k in range(ref.shape[0])], axis=-1)


def chain(faces, place, length, axis):
    inner = (place >= 1) & (place <= length - 3)
    right = jnp.where(inner, faces, 0.0)
    left = moved(right, 1, axis)
    to_first = jnp.where(place == 1, moved(faces, 1, axis), 0.0)
    to_last = jnp.where(place == length - 2, faces, 0.0)
    return left, right, to_first, to_last


def half_sums(arrays, levels):
    wide = jnp.concatenate(arrays, axis=1)
    lanes = arrays[0].shape[1]
    width = lanes // levels
    shape = (8 * levels, wide.shape[1])
    row, col = iota(shape, 0), iota(shape, 1)
    pick = ((col // lanes == row % 8) & (col % lanes // width == row // 8)).astype(F32)
    sums = lax.dot_general(pick, wide, (((1,), (1,)), ((), ())), precision=EXACT, preferred_element_type=F32)
    return jnp.concatenate([sums[8 * k : 8 * k + 8] for k in range(levels)], axis=1)


def padded(rows, lanes):
    return jnp.concatenate([rows, jnp.zeros((rows.shape[0], lanes - rows.shape[1]), F32)], axis=1)


def fetch(sources, buffers, semaphores):
    copies = [
        pltpu.make_async_copy(source, buffer, semaphores.at[k])
        for k, (source, buffer) in enumerate(zip(sources, buffers))
    ]
    for copy in copies:
        copy.start()
    for copy in copies:
        copy.wait()


def zonal_block(field, gamma, kappa_zonal, ocean):
    levels, height, width = field.shape
    place = iota((height, levels * width), 1) % width
    scaled = beside(gamma) * ocean
    source = scaled * beside(field)
    open_face = beside(kappa_zonal) * ocean
    faces = open_face * moved(ocean, -1, 1)
    left, right, to_first, to_last = chain(faces, place, width, 1)
    inner = (place >= 1) & (place <= width - 2)
    factors, (ground, first, last, direct) = condense(
        left,
        right,
        [1.0 + to_first + to_last, to_first, to_last, jnp.where(inner, source, 0.0)],
        width - 2,
        1,
    )
    inverse = jnp.where(inner, 1.0 / ground, 0.0)
    first = first * inverse
    last = last * inverse
    edge = to_first * last
    first = jnp.where(place == 0, 1.0, first)
    last = jnp.where(place == width - 1, 1.0, last)
    outward = jnp.where(place == width - 1, open_face, 0.0)
    terms = [first * source, first, edge, last * source, last, outward]
    return factors, scaled, inverse, direct * inverse, first, last, terms


def unpack(refs, count):
    sources, outputs, buffers, semaphores = refs[:7], refs[7 : 7 + count], refs[7 + count : 14 + count], refs[14 + count]
    fetch(sources, buffers, semaphores)
    return outputs, buffers


def fold_sum(pairing, width):
    return pairing[0] + lax.axis_index("lon") * width


def block_local(*refs):
    (message, payload, factors_out, keep, turn), buffers = unpack(refs, 5)
    field, gamma, kappa_zonal, kappa_merid, area, mask, pairing = buffers
    levels, height, width = field.shape
    ocean_one = mask[...].astype(F32)
    ocean = jnp.concatenate([ocean_one] * levels, axis=1)
    factors, scaled, inverse, direct, first, last, terms = zonal_block(field, gamma, kappa_zonal, ocean)
    place = iota(first.shape, 1) % width
    order = [terms[0], terms[3], terms[1], terms[4], terms[2], terms[5]]
    rows = half_sums(order + [jnp.where(place == 0, ocean, 0.0)], levels)
    message[...] = jnp.broadcast_to(jnp.concatenate([rows[:4], rows[4:]], axis=1)[None], message.shape)
    payload[0] = direct
    payload[1] = first
    payload[2] = last
    payload[3] = beside(kappa_merid) * ocean
    payload[4] = jnp.concatenate([1.0 / area[...], ocean_one], axis=1)
    store_factors(factors_out, factors)
    keep[0] = first
    keep[1] = last
    keep[2] = inverse
    keep[3] = scaled
    turn[...] = jnp.full(turn.shape, fold_sum(pairing, width), jnp.int32)


def ring_setup(first_ground, last_ground, edge, open_face, ocean):
    face = open_face * moved(ocean, -1, 0)
    last_pull = 1.0 / (last_ground + edge + face)
    edge_pull, face_pull = edge * last_pull, face * last_pull
    ground = first_ground + edge_pull * last_ground + moved(face_pull * last_ground, 1, 0)
    link = edge * face_pull
    factors, (ground,) = condense(moved(link, 1, 0), link, [ground], edge.shape[0], 0)
    return edge_pull, face_pull, last_pull, factors, 1.0 / ground


def ring_ends(first_source, last_source, edge_pull, face_pull, last_pull, factors, inverse):
    values = first_source + edge_pull * last_source + moved(face_pull * last_source, 1, 0)
    first = relax(values, factors, 0) * inverse
    last = last_pull * last_source + edge_pull * first + face_pull * moved(first, -1, 0)
    return first, last


def own_row(values, index):
    return jnp.sum(jnp.where(iota(values.shape, 0) == index, values, 0.0), axis=0, keepdims=True)


def columns(own, block, height, levels, lanes):
    width = lanes // levels
    row, col = iota((height, lanes), 0), iota((height, lanes), 1)
    result = None
    for k in range(levels):
        base = (block * levels + k) * height
        group = own[:, base // lanes * lanes : base // lanes * lanes + lanes]
        column = jnp.sum(jnp.where(col == row + base % lanes, group, 0.0), axis=1, keepdims=True)
        result = jnp.broadcast_to(column, (height, lanes)) if k == 0 else jnp.where(col >= k * width, column, result)
    return result


def column_join(gathered, payload, keep, kept, message):
    levels = 2
    devices_y, _, height, lanes = payload.shape
    lines = levels * height
    index_x, index_y = lax.axis_index("lon"), lax.axis_index("lat")
    half = lanes // 2

    def quantity(k):
        lane = k // 4 * half
        return jnp.concatenate(
            [gathered[:, y, k % 4, :][:, lane : lane + lines] for y in range(devices_y)], axis=1
        )

    first_source, last_source, first_ground, last_ground, edge, open_face, ocean = [quantity(k) for k in range(7)]
    ring = ring_setup(first_ground, last_ground, edge, open_face, ocean)
    first_ends, last_ends = ring_ends(first_source, last_source, *ring)
    first_ends, last_ends = own_row(first_ends, index_x), own_row(last_ends, index_x)
    current = jnp.concatenate(
        [
            payload[y, 0]
            + payload[y, 1] * columns(first_ends, y, height, levels, lanes)
            + payload[y, 2] * columns(last_ends, y, height, levels, lanes)
            for y in range(devices_y)
        ],
        axis=0,
    )
    open_face = jnp.concatenate([payload[y, 3] for y in range(devices_y)], axis=0)
    packed = jnp.concatenate([payload[y, 4] for y in range(devices_y)], axis=0)
    reciprocal = jnp.concatenate([packed[:, :half]] * levels, axis=1)
    ocean = jnp.concatenate([packed[:, half:]] * levels, axis=1)
    count = devices_y * height
    row = iota((count, lanes), 0)
    top = row == count - 1
    faces = jnp.where(top, 0.0, open_face * moved(ocean, -1, 0))
    factors, (ground, current, reach) = condense(
        moved(faces, 1, 0), faces, [jnp.ones_like(faces), current, top.astype(F32)], count, 0
    )
    inverse = 1.0 / ground
    current = current * inverse
    reach = reach * inverse
    again = relax(jnp.where(top, 0.0, current * reciprocal), factors, 0) * inverse

    def own_block(values):
        chosen = values[:height]
        for y in range(1, devices_y):
            chosen = jnp.where(index_y == y, values[y * height : (y + 1) * height], chosen)
        return chosen

    again, reach = own_block(again), own_block(reach)
    kept[0] = again
    kept[1] = reach
    rows = half_sums([keep[0] * again, keep[1] * again], levels)
    whole = jnp.concatenate(
        [
            keep[0] * reach,
            keep[1] * reach,
            jnp.concatenate([rows[:1], rows[1:2]], axis=1),
            current[count - 1 :],
            reciprocal[count - 1 :],
            jnp.zeros((5, lanes), F32),
        ],
        axis=0,
    )
    message[...] = jnp.broadcast_to(whole[None], message.shape)


def mirrored(rows, pivot, width):
    devices, lanes = rows[0].shape
    block, lane = iota((devices, lanes), 0), iota((devices, lanes), 1)
    place = lane % width
    pivot_block, pivot_place = pivot // width % devices, pivot % width
    reach = lane - place + (pivot_place - place + width) % width
    wanted = (pivot_block - block - (place > pivot_place).astype(jnp.int32) + 2 * devices) % devices
    results = []
    for values in rows:
        turned = jnp.take_along_axis(values, reach, axis=1)
        result = turned
        for b in range(devices):
            result = jnp.where(wanted == b, turned[b : b + 1], result)
        results.append(result)
    return results


def zonal_close(gathered, ring_rows, kept, factors_ref, keep, turn, out):
    levels, height, width = out.shape
    lanes = levels * width
    lines = levels * height
    half = lanes // 2
    devices = gathered.shape[0]
    index_x, index_y = lax.axis_index("lon"), lax.axis_index("lat")
    mine = ring_rows[:, pl.ds(index_y, 1), :, :].reshape(devices, 4, lanes)
    ring = ring_setup(
        mine[:, 2, :lines],
        mine[:, 3, :lines],
        mine[:, 0, half : half + lines],
        mine[:, 1, half : half + lines],
        mine[:, 2, half : half + lines],
    )
    top, reciprocal = gathered[:, lines + 1, :], gathered[:, lines + 2, :]
    top_across, reciprocal_across = mirrored([top, reciprocal], turn[:devices], width)
    folded = 0.25 * (top + top_across) * (reciprocal + reciprocal_across)
    tiled = jnp.concatenate([folded] * devices, axis=1)
    row, col = iota(tiled.shape, 0), iota(tiled.shape, 1)
    picks = jnp.concatenate(
        [jnp.where((col // lanes == row) & (col % lanes // width == k), tiled, 0.0) for k in range(levels)], axis=0
    )
    reach = jnp.concatenate([gathered[b, : 2 * height, :] for b in range(devices)], axis=1)
    change = lax.dot_general(
        picks, reach, (((1,), (1,)), ((), ())), precision=EXACT, preferred_element_type=F32
    )
    change = [change[k * devices : (k + 1) * devices] for k in range(levels)]
    first_source = gathered[:, lines, :][:, :lines] + jnp.concatenate([c[:, :height] for c in change], axis=1)
    last_source = gathered[:, lines, :][:, half : half + lines] + jnp.concatenate(
        [c[:, height:] for c in change], axis=1
    )
    first_ends, last_ends = ring_ends(first_source, last_source, *ring)
    current = kept[0] + kept[1] * own_row(folded, index_x)
    inner = keep[2] > 0.0
    direct = relax(jnp.where(inner, current, 0.0), load_factors(factors_ref), 1) * keep[2]

    result = keep[3] * (
        direct
        + keep[0] * spread_ends(first_ends, index_x, height, levels, lanes)
        + keep[1] * spread_ends(last_ends, index_x, height, levels, lanes)
    )
    for k in range(levels):
        out[k] = result[:, k * width : (k + 1) * width]


def run(body, shapes, *operands, outside=False, scratch=()):
    vmem = pl.BlockSpec(memory_space=pltpu.VMEM)
    hbm = pl.BlockSpec(memory_space=pltpu.HBM)
    if outside:
        operands = [pltpu.with_memory_space_constraint(x, pltpu.HBM) for x in operands]
    return pl.pallas_call(
        body,
        out_shape=shapes,
        in_specs=[hbm if outside else vmem] * len(operands),
        out_specs=[vmem] * len(shapes),
        scratch_shapes=scratch,
        compiler_params=pltpu.CompilerParams(vmem_limit_bytes=8 << 20),
        name=body.__name__,
    )(*operands)


def array(*shape, dtype=F32):
    return jax.ShapeDtypeStruct(shape, dtype)


def column_order(place, width):
    return jnp.where(place < width // 2, place, width + width // 2 - 1 - place)


def block_send(*refs):
    (message, factors_out, keep, turn), buffers = unpack(refs, 4)
    field, gamma, kappa_zonal, kappa_merid, area, mask, pairing = buffers
    levels, height, width = field.shape
    lanes = levels * width
    half = width // 2
    ocean_one = mask[...].astype(F32)
    ocean = jnp.concatenate([ocean_one] * levels, axis=1)
    factors, scaled, inverse, direct, first, last, terms = zonal_block(field, gamma, kappa_zonal, ocean)
    devices = message.shape[0]
    centre = (fold_sum(pairing, width) % (lax.axis_size("lon") * width) + 1) // 2
    row = iota((height, lanes), 0)
    merid = beside(kappa_merid) * jnp.where(row == height - 1, ocean, ocean * moved(ocean, -1, 0))
    lane = iota((height, lanes), 1)
    reach = lane // width * width + (column_order(lane % width, width) + centre) % width

    def ordered(values):
        return jnp.take_along_axis(values, reach, axis=1)

    pieces = jnp.concatenate([ordered(x) for x in (direct, first, last, merid)], axis=0).T
    for k, start in enumerate((0, width, half, width + half)):
        message[:, k, :] = pieces[start : start + devices]
    packed = ordered(jnp.concatenate([1.0 / area[...], ocean_one], axis=1))

    def tile(distance):
        return jnp.broadcast_to(moved(packed, distance, 1)[:1], (8, lanes))

    extra = jnp.concatenate(
        [
            packed,
            jnp.broadcast_to(ocean_one[:, :1], (height, lanes)),
            tile(-width - half),
            moved(packed, -half, 1),
            jnp.zeros((lanes - 3 * height - 16, lanes), F32),
            tile(-width),
        ],
        axis=0,
    ).T
    message[:, 4, :] = extra[:devices]
    wide = jnp.concatenate([terms[0], terms[3], terms[2], terms[5]], axis=0).T
    sums = level_sums(wide, levels)
    grounds = level_sums(pieces, levels)
    middle = iota((1, lanes), 1) // height
    grounds = jnp.where((middle == 1) | (middle == 2), grounds[0], moved(grounds[1], 2 * height, 1))
    for k, values in enumerate((*sums, grounds)):
        message[:, 5 + k, :] = jnp.broadcast_to(values, (devices, lanes))
    store_factors(factors_out, factors)
    keep[0] = first
    keep[1] = last
    keep[2] = inverse
    keep[3] = scaled
    turn[...] = jnp.full(turn.shape, centre, jnp.int32)


def level_sums(values, levels):
    part = values.shape[0] // levels
    return [jnp.sum(values[k * part : (k + 1) * part], axis=0, keepdims=True) for k in range(levels)]


def ring_place(k, level):
    return (5 + level, k) if k < 4 else (7, (1 + k - 4 + 2 * level) % 4)


def column_solve(gathered, turn, message, hold):
    devices_x, devices_y, tall, lanes = gathered.shape
    height = lanes // devices_y
    width = devices_x * devices_y * 2
    levels = 2
    pairs = devices_x // 2
    shape = (pairs * tall, lanes)
    small = iota((devices_x, lanes), 1) // height
    lane = iota(shape, 1)
    line = iota(shape, 0) % tall
    lower = line < 4
    outer = line % 4 < 2
    lats = range(devices_y)

    def merged(parts, where, target):
        result = None
        for k, values in enumerate(parts):
            turned = moved(values, (k - where[k]) * height, 1)
            result = turned if k == 0 else jnp.where(target == k, turned, result)
        return result

    def ring_term(k):
        parts = []
        for level in range(levels):
            r, group = ring_place(k, level)
            parts.append(merged([gathered[:, y, r, :] for y in lats], [group] * devices_y, small))
        return jnp.concatenate(parts, axis=1)

    first_source, last_source, edge, open_face, first_ground, last_ground = [ring_term(k) for k in range(6)]
    ocean = merged([gathered[:, y, 4, :] for y in lats], [1] * devices_y, small)
    ring = ring_setup(first_ground, last_ground, edge, open_face, jnp.concatenate([ocean] * levels, axis=1))
    first_ends, last_ends = ring_ends(first_source, last_source, *ring)

    def at_columns(ends):
        row = iota((tall, lanes), 0)
        tiles = []
        for b in range(pairs):
            near, far = ends[b : b + 1], ends[b + pairs : b + pairs + 1]
            even = jnp.where(row < 4, near[:, :lanes], far[:, :lanes])
            odd = jnp.where(row < 4, near[:, lanes:], far[:, lanes:])
            tiles.append(jnp.where(row % levels == 0, even, odd))
        return jnp.concatenate(tiles, axis=0)

    def paired(values):
        near, far = values[:pairs].reshape(shape), values[pairs:].reshape(shape)
        return jnp.where(lower, near, moved(far, 4, 0))

    tiles = [paired(gathered[:, y, :, :]) for y in lats]
    direct, first, last, faces = [merged(tiles, [k] * devices_y, lane // height) for k in range(4)]
    current = direct + first * at_columns(first_ends) + last * at_columns(last_ends)
    reciprocal, beyond = None, jnp.zeros(shape, F32)
    for y in lats:
        near, far = [
            jnp.broadcast_to(gathered[k : k + pairs, y, 4:5, :], (pairs, tall, lanes)).reshape(shape)
            for k in (0, pairs)
        ]
        extra = jnp.where(lower, near, far)
        turned = jnp.where(outer, moved(extra, y * height, 1), moved(extra, (y - 2) * height - 8, 1))
        reciprocal = turned if y == 0 else jnp.where(lane // height == y, turned, reciprocal)
        if y > 0:
            beyond = jnp.where(lane == y * height - 1, turned, beyond)
    faces = jnp.where(lane % height == height - 1, faces * beyond, faces)
    factors, (ground, current) = condense(
        moved(faces, 1, 1), faces, [jnp.ones(shape, F32), current], lanes, 1
    )
    inverse = 1.0 / ground
    current = current * inverse

    index = lax.axis_index("lon") * devices_y + lax.axis_index("lat")
    centre = turn[...]
    block, place = centre // width, centre % width
    offset = devices_x - 1 + 2 * block
    offset = offset + (index + place >= width).astype(jnp.int32) + (place - 1 - index >= 0).astype(jnp.int32)

    def across(values):
        parts = []
        for b in range(pairs):
            wanted = (offset - b + devices_x) % devices_x
            part = values[:tall]
            for k in range(1, pairs):
                part = jnp.where(wanted % pairs == k, values[k * tall : (k + 1) * tall], part)
            parts.append(jnp.where(wanted >= pairs, moved(part, 4, 0), part))
        other = jnp.concatenate(parts, axis=0)
        return jnp.where(outer, moved(other, -2, 0), moved(other, 2, 0))

    folded = 0.25 * (current + across(current)) * (reciprocal + across(reciprocal))
    current = jnp.where(lane == lanes - 1, folded, current * reciprocal)
    current = relax(current, factors, 1) * inverse

    first, last = first * current, last * current
    first, last = first + moved(first, -2, 0), last + moved(last, -2, 0)
    for k, values in enumerate((jnp.where(outer, first, moved(last, 2, 0)), current)):
        for b in range(pairs):
            tile = values[b * tall : (b + 1) * tall]
            hold[k, b] = tile
            hold[k, b + pairs] = moved(tile, 4, 0)
    sources = [jnp.concatenate([hold[0, :, k, :], hold[0, :, k + 1, :]], axis=1) for k in (0, 2)]
    ends = ring_ends(*sources, *ring)
    ends = [part[:, k * lanes : (k + 1) * lanes] for part in ends for k in range(levels)]
    own = [hold[1, :, k, :] for k in range(4)]
    for y in lats:
        message[:, y, 0, :] = merged(own, [y] * 4, small)
        message[:, y, 1, :] = merged(ends, [y] * 4, small)


def block_close(gathered, factors_ref, keep, turn, out):
    levels, height, width = out.shape
    lanes = levels * width
    own, ends = gathered[:, 0, :], jnp.sum(gathered[:, 1, :], axis=0, keepdims=True)
    turned = jnp.concatenate([moved(own, -k * height, 1) for k in (0, 2, 1, 3)], axis=0).T[:height]
    lane = iota((height, lanes), 1)
    centre = jnp.broadcast_to(turn[:1], (height, lanes))
    reach = lane // width * width + column_order((lane - centre + 8 * width) % width, width)
    current = jnp.take_along_axis(turned, reach, axis=1)
    inner = keep[2] > 0.0
    direct = relax(jnp.where(inner, current, 0.0), load_factors(factors_ref), 1) * keep[2]
    first, last = [columns(ends, k, height, levels, lanes) for k in range(2)]
    result = keep[3] * (direct + keep[0] * first + keep[1] * last)
    for k in range(levels):
        out[k] = result[:, k * width : (k + 1) * width]


def spread_ends(values, index, height, levels, lanes):
    own = own_row(values, index)
    return columns(jnp.concatenate([own, own], axis=1)[:, :lanes], 0, height, levels, lanes)


def local_by_columns(operands, scratch, count):
    levels, height, width = operands[0].shape
    lanes = levels * width
    devices_x, devices_y = lax.axis_size("lon"), lax.axis_size("lat")
    devices = devices_x * devices_y
    message, factors, keep, turn = run(
        block_send,
        [
            array(devices, 8, lanes),
            array(count, height, lanes),
            array(4, height, lanes),
            array(8, lanes, dtype=jnp.int32),
        ],
        *operands,
        outside=True,
        scratch=scratch,
    )
    both = ("lon", "lat")
    ring_rows = lax.all_to_all(message, both, split_axis=0, concat_axis=0, tiled=True)
    ring_rows = ring_rows.reshape(devices_x, devices_y, 8, lanes)
    (message,) = run(
        column_solve,
        [array(devices_x, devices_y, 2, lanes)],
        ring_rows,
        turn,
        scratch=[pltpu.VMEM((2, devices_x, 8, lanes), F32)],
    )
    message = message.reshape(devices, 2, lanes)
    gathered = lax.all_to_all(message, both, split_axis=0, concat_axis=0, tiled=True)
    (result,) = run(block_close, [array(levels, height, width)], gathered, factors, keep, turn)
    return result


def local(field, gamma, kappa_zonal, kappa_merid, area, sea_mask, fold_pair):
    levels, height, width = field.shape
    lanes = levels * width
    devices_x, devices_y = lax.axis_size("lon"), lax.axis_size("lat")
    count = 2 * (width - 3).bit_length()
    operands = (field, gamma, kappa_zonal, kappa_merid, area, sea_mask, fold_pair)
    scratch = [pltpu.VMEM(x.shape, x.dtype) for x in operands[:-1]]
    scratch += [pltpu.SMEM(fold_pair.shape, fold_pair.dtype), pltpu.SemaphoreType.DMA((len(operands),))]
    if width == 2 * devices_x * devices_y and levels == 2 and devices_y * height == lanes == 4 * height:
        return local_by_columns(operands, scratch, count)
    message, payload, factors, keep, turn = run(
        block_local,
        [
            array(devices_x * devices_y, 4, lanes),
            array(5, height, lanes),
            array(count, height, lanes),
            array(4, height, lanes),
            array(devices_x, lanes, dtype=jnp.int32),
        ],
        *operands,
        outside=True,
        scratch=scratch,
    )
    ring_rows = lax.all_to_all(message, ("lon", "lat"), split_axis=0, concat_axis=0, tiled=True)
    ring_rows = ring_rows.reshape(devices_x, devices_y, 4, lanes)
    payload = lax.all_gather(payload, "lat", axis=0, tiled=False)
    kept, message = run(
        column_join,
        [array(2, height, lanes), array(devices_x, 2 * height + 8, lanes)],
        ring_rows, payload, keep,
    )
    gathered = lax.all_to_all(message, "lon", split_axis=0, concat_axis=0, tiled=True)
    (result,) = run(
        zonal_close, [array(levels, height, width)], gathered, ring_rows, kept, factors, keep, turn
    )
    return result


def solution(mesh):
    blocks = P(None, "lat", "lon")
    return jax.shard_map(
        local,
        mesh=mesh,
        in_specs=(blocks, blocks, blocks, blocks, P("lat", "lon"), P("lat", "lon"), P("lon")),
        out_specs=blocks,
        check_vma=False,
    )
```

```python
import functools

import jax
import jax.numpy as jnp
from jax import lax
from jax.experimental import pallas as pl
from jax.experimental.pallas import tpu as pltpu
from jax.sharding import PartitionSpec as P


F32 = jnp.float32
EXACT = lax.Precision.HIGHEST


def moved(values, distance, axis):
    distance %= values.shape[axis]
    return pltpu.roll(values, distance, axis) if distance else values


def iota(shape, axis):
    return lax.broadcasted_iota(jnp.int32, shape, axis)


def spread(values, up, down, stride, axis):
    return values + moved(up * values, stride, axis) + moved(down * values, -stride, axis)


def condense(left, right, totals, count, axis):
    factors = []
    stride = 1
    while stride < count:
        pull = 1.0 / (totals[0] + left + right)
        up, down = right * pull, left * pull
        link = left * up
        factors.append((up, down))
        totals = [spread(t, up, down, stride, axis) for t in totals]
        left, right = moved(link, stride, axis), moved(link, -stride, axis)
        stride *= 2
    return factors, totals


def relax(values, factors, axis):
    stride = 1
    for up, down in factors:
        values = spread(values, up, down, stride, axis)
        stride *= 2
    return values


def relax_by_pairs(values, factors, axis):
    stride = 1
    for k in range(0, len(factors), 2):
        if k + 1 == len(factors):
            return spread(values, *factors[k], stride, axis)
        (up, down), (far_up, far_down) = factors[k : k + 2]
        reach = {
            3: moved(far_up, -stride, axis) * up,
            2: far_up,
            1: up + moved(far_up, stride, axis) * down,
            -1: down + moved(far_down, -stride, axis) * up,
            -2: far_down,
            -3: moved(far_down, stride, axis) * down,
        }
        parts = [moved(factor * values, n * stride, axis) for n, factor in reach.items()]
        values = (values + parts[1]) + (parts[0] + parts[2]) + ((parts[3] + parts[4]) + parts[5])
        stride *= 4
    return values


def load_factors(ref):
    return [(ref[2 * k], ref[2 * k + 1]) for k in range(ref.shape[0] // 2)]


def store_factors(ref, factors):
    for k, (up, down) in enumerate(factors):
        ref[2 * k] = up
        ref[2 * k + 1] = down


def beside(ref):
    return jnp.concatenate([ref[k] for k in range(ref.shape[0])], axis=-1)


def chain(faces, place, length, axis):
    inner = (place >= 1) & (place <= length - 3)
    right = jnp.where(inner, faces, 0.0)
    left = moved(right, 1, axis)
    to_first = jnp.where(place == 1, moved(faces, 1, axis), 0.0)
    to_last = jnp.where(place == length - 2, faces, 0.0)
    return left, right, to_first, to_last


def half_sums(arrays, levels):
    wide = jnp.concatenate(arrays, axis=1)
    lanes = arrays[0].shape[1]
    width = lanes // levels
    shape = (8 * levels, wide.shape[1])
    row, col = iota(shape, 0), iota(shape, 1)
    pick = ((col // lanes == row % 8) & (col % lanes // width == row // 8)).astype(F32)
    sums = lax.dot_general(pick, wide, (((1,), (1,)), ((), ())), precision=EXACT, preferred_element_type=F32)
    return jnp.concatenate([sums[8 * k : 8 * k + 8] for k in range(levels)], axis=1)


def padded(rows, lanes):
    return jnp.concatenate([rows, jnp.zeros((rows.shape[0], lanes - rows.shape[1]), F32)], axis=1)


def fetch(sources, buffers, semaphores):
    copies = [
        pltpu.make_async_copy(source, buffer, semaphores.at[k])
        for k, (source, buffer) in enumerate(zip(sources, buffers))
    ]
    for copy in copies:
        copy.start()
    for copy in copies:
        copy.wait()


def zonal_block(field, gamma, kappa_zonal, ocean):
    levels, height, width = field.shape
    place = iota((height, levels * width), 1) % width
    scaled = beside(gamma) * ocean
    source = scaled * beside(field)
    open_face = beside(kappa_zonal) * ocean
    faces = open_face * moved(ocean, -1, 1)
    left, right, to_first, to_last = chain(faces, place, width, 1)
    inner = (place >= 1) & (place <= width - 2)
    factors, (ground, first, last, direct) = condense(
        left,
        right,
        [1.0 + to_first + to_last, to_first, to_last, jnp.where(inner, source, 0.0)],
        width - 2,
        1,
    )
    inverse = jnp.where(inner, 1.0 / ground, 0.0)
    first = first * inverse
    last = last * inverse
    edge = to_first * last
    first = jnp.where(place == 0, 1.0, first)
    last = jnp.where(place == width - 1, 1.0, last)
    outward = jnp.where(place == width - 1, open_face, 0.0)
    terms = [first * source, first, edge, last * source, last, outward]
    return factors, scaled, inverse, direct * inverse, first, last, terms


def unpack(refs, count):
    sources, outputs, buffers, semaphores = refs[:7], refs[7 : 7 + count], refs[7 + count : 14 + count], refs[14 + count]
    fetch(sources, buffers, semaphores)
    return outputs, buffers


def fold_sum(pairing, width):
    return pairing[0] + lax.axis_index("lon") * width


def block_local(*refs):
    (message, payload, factors_out, keep, turn), buffers = unpack(refs, 5)
    field, gamma, kappa_zonal, kappa_merid, area, mask, pairing = buffers
    levels, height, width = field.shape
    ocean_one = mask[...].astype(F32)
    ocean = jnp.concatenate([ocean_one] * levels, axis=1)
    factors, scaled, inverse, direct, first, last, terms = zonal_block(field, gamma, kappa_zonal, ocean)
    place = iota(first.shape, 1) % width
    order = [terms[0], terms[3], terms[1], terms[4], terms[2], terms[5]]
    rows = half_sums(order + [jnp.where(place == 0, ocean, 0.0)], levels)
    message[...] = jnp.broadcast_to(jnp.concatenate([rows[:4], rows[4:]], axis=1)[None], message.shape)
    payload[0] = direct
    payload[1] = first
    payload[2] = last
    payload[3] = beside(kappa_merid) * ocean
    payload[4] = jnp.concatenate([1.0 / area[...], ocean_one], axis=1)
    store_factors(factors_out, factors)
    keep[0] = first
    keep[1] = last
    keep[2] = inverse
    keep[3] = scaled
    turn[...] = jnp.full(turn.shape, fold_sum(pairing, width), jnp.int32)


def ring_setup(first_ground, last_ground, edge, open_face, ocean):
    face = open_face * moved(ocean, -1, 0)
    last_pull = 1.0 / (last_ground + edge + face)
    edge_pull, face_pull = edge * last_pull, face * last_pull
    ground = first_ground + edge_pull * last_ground + moved(face_pull * last_ground, 1, 0)
    link = edge * face_pull
    factors, (ground,) = condense(moved(link, 1, 0), link, [ground], edge.shape[0], 0)
    return edge_pull, face_pull, last_pull, factors, 1.0 / ground


def ring_ends(first_source, last_source, edge_pull, face_pull, last_pull, factors, inverse):
    values = first_source + edge_pull * last_source + moved(face_pull * last_source, 1, 0)
    first = relax(values, factors, 0) * inverse
    last = last_pull * last_source + edge_pull * first + face_pull * moved(first, -1, 0)
    return first, last


def own_row(values, index):
    return jnp.sum(jnp.where(iota(values.shape, 0) == index, values, 0.0), axis=0, keepdims=True)


def columns(own, block, height, levels, lanes):
    width = lanes // levels
    row, col = iota((height, lanes), 0), iota((height, lanes), 1)
    result = None
    for k in range(levels):
        base = (block * levels + k) * height
        group = own[:, base // lanes * lanes : base // lanes * lanes + lanes]
        column = jnp.sum(jnp.where(col == row + base % lanes, group, 0.0), axis=1, keepdims=True)
        result = jnp.broadcast_to(column, (height, lanes)) if k == 0 else jnp.where(col >= k * width, column, result)
    return result


def column_join(gathered, payload, keep, kept, message):
    levels = 2
    devices_y, _, height, lanes = payload.shape
    lines = levels * height
    index_x, index_y = lax.axis_index("lon"), lax.axis_index("lat")
    half = lanes // 2

    def quantity(k):
        lane = k // 4 * half
        return jnp.concatenate(
            [gathered[:, y, k % 4, :][:, lane : lane + lines] for y in range(devices_y)], axis=1
        )

    first_source, last_source, first_ground, last_ground, edge, open_face, ocean = [quantity(k) for k in range(7)]
    ring = ring_setup(first_ground, last_ground, edge, open_face, ocean)
    first_ends, last_ends = ring_ends(first_source, last_source, *ring)
    first_ends, last_ends = own_row(first_ends, index_x), own_row(last_ends, index_x)
    current = jnp.concatenate(
        [
            payload[y, 0]
            + payload[y, 1] * columns(first_ends, y, height, levels, lanes)
            + payload[y, 2] * columns(last_ends, y, height, levels, lanes)
            for y in range(devices_y)
        ],
        axis=0,
    )
    open_face = jnp.concatenate([payload[y, 3] for y in range(devices_y)], axis=0)
    packed = jnp.concatenate([payload[y, 4] for y in range(devices_y)], axis=0)
    reciprocal = jnp.concatenate([packed[:, :half]] * levels, axis=1)
    ocean = jnp.concatenate([packed[:, half:]] * levels, axis=1)
    count = devices_y * height
    row = iota((count, lanes), 0)
    top = row == count - 1
    faces = jnp.where(top, 0.0, open_face * moved(ocean, -1, 0))
    factors, (ground, current, reach) = condense(
        moved(faces, 1, 0), faces, [jnp.ones_like(faces), current, top.astype(F32)], count, 0
    )
    inverse = 1.0 / ground
    current = current * inverse
    reach = reach * inverse
    again = relax(jnp.where(top, 0.0, current * reciprocal), factors, 0) * inverse

    def own_block(values):
        chosen = values[:height]
        for y in range(1, devices_y):
            chosen = jnp.where(index_y == y, values[y * height : (y + 1) * height], chosen)
        return chosen

    again, reach = own_block(again), own_block(reach)
    kept[0] = again
    kept[1] = reach
    rows = half_sums([keep[0] * again, keep[1] * again], levels)
    whole = jnp.concatenate(
        [
            keep[0] * reach,
            keep[1] * reach,
            jnp.concatenate([rows[:1], rows[1:2]], axis=1),
            current[count - 1 :],
            reciprocal[count - 1 :],
            jnp.zeros((5, lanes), F32),
        ],
        axis=0,
    )
    message[...] = jnp.broadcast_to(whole[None], message.shape)


def mirrored(rows, pivot, width):
    devices, lanes = rows[0].shape
    block, lane = iota((devices, lanes), 0), iota((devices, lanes), 1)
    place = lane % width
    pivot_block, pivot_place = pivot // width % devices, pivot % width
    reach = lane - place + (pivot_place - place + width) % width
    wanted = (pivot_block - block - (place > pivot_place).astype(jnp.int32) + 2 * devices) % devices
    results = []
    for values in rows:
        turned = jnp.take_along_axis(values, reach, axis=1)
        result = turned
        for b in range(devices):
            result = jnp.where(wanted == b, turned[b : b + 1], result)
        results.append(result)
    return results


def zonal_close(gathered, ring_rows, kept, factors_ref, keep, turn, out):
    levels, height, width = out.shape
    lanes = levels * width
    lines = levels * height
    half = lanes // 2
    devices = gathered.shape[0]
    index_x, index_y = lax.axis_index("lon"), lax.axis_index("lat")
    mine = ring_rows[:, pl.ds(index_y, 1), :, :].reshape(devices, 4, lanes)
    ring = ring_setup(
        mine[:, 2, :lines],
        mine[:, 3, :lines],
        mine[:, 0, half : half + lines],
        mine[:, 1, half : half + lines],
        mine[:, 2, half : half + lines],
    )
    top, reciprocal = gathered[:, lines + 1, :], gathered[:, lines + 2, :]
    top_across, reciprocal_across = mirrored([top, reciprocal], turn[:devices], width)
    folded = 0.25 * (top + top_across) * (reciprocal + reciprocal_across)
    tiled = jnp.concatenate([folded] * devices, axis=1)
    row, col = iota(tiled.shape, 0), iota(tiled.shape, 1)
    picks = jnp.concatenate(
        [jnp.where((col // lanes == row) & (col % lanes // width == k), tiled, 0.0) for k in range(levels)], axis=0
    )
    reach = jnp.concatenate([gathered[b, : 2 * height, :] for b in range(devices)], axis=1)
    change = lax.dot_general(
        picks, reach, (((1,), (1,)), ((), ())), precision=EXACT, preferred_element_type=F32
    )
    change = [change[k * devices : (k + 1) * devices] for k in range(levels)]
    first_source = gathered[:, lines, :][:, :lines] + jnp.concatenate([c[:, :height] for c in change], axis=1)
    last_source = gathered[:, lines, :][:, half : half + lines] + jnp.concatenate(
        [c[:, height:] for c in change], axis=1
    )
    first_ends, last_ends = ring_ends(first_source, last_source, *ring)
    current = kept[0] + kept[1] * own_row(folded, index_x)
    inner = keep[2] > 0.0
    direct = relax(jnp.where(inner, current, 0.0), load_factors(factors_ref), 1) * keep[2]

    result = keep[3] * (
        direct
        + keep[0] * spread_ends(first_ends, index_x, height, levels, lanes)
        + keep[1] * spread_ends(last_ends, index_x, height, levels, lanes)
    )
    for k in range(levels):
        out[k] = result[:, k * width : (k + 1) * width]


def run(body, shapes, *operands, outside=False, scratch=()):
    vmem = pl.BlockSpec(memory_space=pltpu.VMEM)
    hbm = pl.BlockSpec(memory_space=pltpu.HBM)
    if outside:
        operands = [pltpu.with_memory_space_constraint(x, pltpu.HBM) for x in operands]
    return pl.pallas_call(
        body,
        out_shape=shapes,
        in_specs=[hbm if outside else vmem] * len(operands),
        out_specs=[vmem] * len(shapes),
        scratch_shapes=scratch,
        compiler_params=pltpu.CompilerParams(vmem_limit_bytes=8 << 20),
        name=body.__name__,
    )(*operands)


def array(*shape, dtype=F32):
    return jax.ShapeDtypeStruct(shape, dtype)


def column_order(place, width):
    return jnp.where(place < width // 2, place, width + width // 2 - 1 - place)


def block_send(*refs):
    (message, factors_out, keep, turn), buffers = unpack(refs, 4)
    field, gamma, kappa_zonal, kappa_merid, area, mask, pairing = buffers
    levels, height, width = field.shape
    lanes = levels * width
    half = width // 2
    ocean_one = mask[...].astype(F32)
    ocean = jnp.concatenate([ocean_one] * levels, axis=1)
    factors, scaled, inverse, direct, first, last, terms = zonal_block(field, gamma, kappa_zonal, ocean)
    devices = message.shape[0]
    centre = (fold_sum(pairing, width) % (lax.axis_size("lon") * width) + 1) // 2
    row = iota((height, lanes), 0)
    merid = beside(kappa_merid) * jnp.where(row == height - 1, ocean, ocean * moved(ocean, -1, 0))
    lane = iota((height, lanes), 1)
    reach = lane // width * width + (column_order(lane % width, width) + centre) % width

    def ordered(values):
        return jnp.take_along_axis(values, reach, axis=1)

    pieces = jnp.concatenate([ordered(x) for x in (direct, first, last, merid)], axis=0).T
    for k, start in enumerate((0, width, half, width + half)):
        message[:, k, :] = pieces[start : start + devices]
    packed = ordered(jnp.concatenate([1.0 / area[...], ocean_one], axis=1))

    def tile(distance):
        return jnp.broadcast_to(moved(packed, distance, 1)[:1], (8, lanes))

    extra = jnp.concatenate(
        [
            packed,
            jnp.broadcast_to(ocean_one[:, :1], (height, lanes)),
            tile(-width - half),
            moved(packed, -half, 1),
            jnp.zeros((lanes - 3 * height - 16, lanes), F32),
            tile(-width),
        ],
        axis=0,
    ).T
    message[:, 4, :] = extra[:devices]
    wide = jnp.concatenate([terms[0], terms[3], terms[2], terms[5]], axis=0).T
    sums = level_sums(wide, levels)
    grounds = level_sums(pieces, levels)
    middle = iota((1, lanes), 1) // height
    grounds = jnp.where((middle == 1) | (middle == 2), grounds[0], moved(grounds[1], 2 * height, 1))
    for k, values in enumerate((*sums, grounds)):
        message[:, 5 + k, :] = jnp.broadcast_to(values, (devices, lanes))
    store_factors(factors_out, factors)
    keep[0] = first
    keep[1] = last
    keep[2] = inverse
    keep[3] = scaled
    turn[...] = jnp.full(turn.shape, centre, jnp.int32)


def level_sums(values, levels):
    part = values.shape[0] // levels
    return [jnp.sum(values[k * part : (k + 1) * part], axis=0, keepdims=True) for k in range(levels)]


def ring_place(k, level):
    return (5 + level, k) if k < 4 else (7, (1 + k - 4 + 2 * level) % 4)


def column_solve(gathered, turn, message, hold):
    devices_x, devices_y, tall, lanes = gathered.shape
    height = lanes // devices_y
    width = devices_x * devices_y * 2
    levels = 2
    pairs = devices_x // 2
    shape = (pairs * tall, lanes)
    small = iota((devices_x, lanes), 1) // height
    lane = iota(shape, 1)
    line = iota(shape, 0) % tall
    lower = line < 4
    outer = line % 4 < 2
    lats = range(devices_y)

    def merged(parts, where, target):
        result = None
        for k, values in enumerate(parts):
            turned = moved(values, (k - where[k]) * height, 1)
            result = turned if k == 0 else jnp.where(target == k, turned, result)
        return result

    def ring_term(k):
        parts = []
        for level in range(levels):
            r, group = ring_place(k, level)
            parts.append(merged([gathered[:, y, r, :] for y in lats], [group] * devices_y, small))
        return jnp.concatenate(parts, axis=1)

    first_source, last_source, edge, open_face, first_ground, last_ground = [ring_term(k) for k in range(6)]
    ocean = merged([gathered[:, y, 4, :] for y in lats], [1] * devices_y, small)
    ring = ring_setup(first_ground, last_ground, edge, open_face, jnp.concatenate([ocean] * levels, axis=1))
    first_ends, last_ends = ring_ends(first_source, last_source, *ring)

    def at_columns(ends):
        row = iota((tall, lanes), 0)
        tiles = []
        for b in range(pairs):
            near, far = ends[b : b + 1], ends[b + pairs : b + pairs + 1]
            even = jnp.where(row < 4, near[:, :lanes], far[:, :lanes])
            odd = jnp.where(row < 4, near[:, lanes:], far[:, lanes:])
            tiles.append(jnp.where(row % levels == 0, even, odd))
        return jnp.concatenate(tiles, axis=0)

    def paired(values):
        near, far = values[:pairs].reshape(shape), values[pairs:].reshape(shape)
        return jnp.where(lower, near, moved(far, 4, 0))

    tiles = [paired(gathered[:, y, :, :]) for y in lats]
    direct, first, last, faces = [merged(tiles, [k] * devices_y, lane // height) for k in range(4)]
    current = direct + first * at_columns(first_ends) + last * at_columns(last_ends)
    reciprocal, beyond = None, jnp.zeros(shape, F32)
    for y in lats:
        near, far = [
            jnp.broadcast_to(gathered[k : k + pairs, y, 4:5, :], (pairs, tall, lanes)).reshape(shape)
            for k in (0, pairs)
        ]
        extra = jnp.where(lower, near, far)
        turned = jnp.where(outer, moved(extra, y * height, 1), moved(extra, (y - 2) * height - 8, 1))
        reciprocal = turned if y == 0 else jnp.where(lane // height == y, turned, reciprocal)
        if y > 0:
            beyond = jnp.where(lane == y * height - 1, turned, beyond)
    faces = jnp.where(lane % height == height - 1, faces * beyond, faces)
    factors, (ground, current) = condense(
        moved(faces, 1, 1), faces, [jnp.ones(shape, F32), current], lanes, 1
    )
    inverse = 1.0 / ground
    current = current * inverse

    index = lax.axis_index("lon") * devices_y + lax.axis_index("lat")
    centre = turn[...]
    block, place = centre // width, centre % width
    offset = devices_x - 1 + 2 * block
    offset = offset + (index + place >= width).astype(jnp.int32) + (place - 1 - index >= 0).astype(jnp.int32)

    def across(values):
        parts = []
        for b in range(pairs):
            wanted = (offset - b + devices_x) % devices_x
            part = values[:tall]
            for k in range(1, pairs):
                part = jnp.where(wanted % pairs == k, values[k * tall : (k + 1) * tall], part)
            parts.append(jnp.where(wanted >= pairs, moved(part, 4, 0), part))
        other = jnp.concatenate(parts, axis=0)
        return jnp.where(outer, moved(other, -2, 0), moved(other, 2, 0))

    folded = 0.25 * (current + across(current)) * (reciprocal + across(reciprocal))
    current = jnp.where(lane == lanes - 1, folded, current * reciprocal)
    current = relax_by_pairs(current, factors, 1) * inverse

    first, last = first * current, last * current
    first, last = first + moved(first, -2, 0), last + moved(last, -2, 0)
    for k, values in enumerate((jnp.where(outer, first, moved(last, 2, 0)), current)):
        for b in range(pairs):
            tile = values[b * tall : (b + 1) * tall]
            hold[k, b] = tile
            hold[k, b + pairs] = moved(tile, 4, 0)
    sources = [jnp.concatenate([hold[0, :, k, :], hold[0, :, k + 1, :]], axis=1) for k in (0, 2)]
    ends = ring_ends(*sources, *ring)
    ends = [part[:, k * lanes : (k + 1) * lanes] for part in ends for k in range(levels)]
    own = [hold[1, :, k, :] for k in range(4)]
    for y in lats:
        message[:, y, 0, :] = merged(own, [y] * 4, small)
        message[:, y, 1, :] = merged(ends, [y] * 4, small)


def block_close(gathered, factors_ref, keep, turn, out):
    levels, height, width = out.shape
    lanes = levels * width
    own, ends = gathered[:, 0, :], jnp.sum(gathered[:, 1, :], axis=0, keepdims=True)
    turned = jnp.concatenate([moved(own, -k * height, 1) for k in (0, 2, 1, 3)], axis=0).T[:height]
    lane = iota((height, lanes), 1)
    centre = jnp.broadcast_to(turn[:1], (height, lanes))
    reach = lane // width * width + column_order((lane - centre + 8 * width) % width, width)
    current = jnp.take_along_axis(turned, reach, axis=1)
    inner = keep[2] > 0.0
    direct = relax_by_pairs(jnp.where(inner, current, 0.0), load_factors(factors_ref), 1) * keep[2]
    first, last = [columns(ends, k, height, levels, lanes) for k in range(2)]
    result = keep[3] * (direct + keep[0] * first + keep[1] * last)
    for k in range(levels):
        out[k] = result[:, k * width : (k + 1) * width]


def spread_ends(values, index, height, levels, lanes):
    own = own_row(values, index)
    return columns(jnp.concatenate([own, own], axis=1)[:, :lanes], 0, height, levels, lanes)


def local_by_columns(operands, scratch, count):
    levels, height, width = operands[0].shape
    lanes = levels * width
    devices_x, devices_y = lax.axis_size("lon"), lax.axis_size("lat")
    devices = devices_x * devices_y
    message, factors, keep, turn = run(
        block_send,
        [
            array(devices, 8, lanes),
            array(count, height, lanes),
            array(4, height, lanes),
            array(8, lanes, dtype=jnp.int32),
        ],
        *operands,
        outside=True,
        scratch=scratch,
    )
    both = ("lon", "lat")
    ring_rows = lax.all_to_all(message, both, split_axis=0, concat_axis=0, tiled=True)
    ring_rows = ring_rows.reshape(devices_x, devices_y, 8, lanes)
    (message,) = run(
        column_solve,
        [array(devices_x, devices_y, 2, lanes)],
        ring_rows,
        turn,
        scratch=[pltpu.VMEM((2, devices_x, 8, lanes), F32)],
    )
    message = message.reshape(devices, 2, lanes)
    gathered = lax.all_to_all(message, both, split_axis=0, concat_axis=0, tiled=True)
    (result,) = run(block_close, [array(levels, height, width)], gathered, factors, keep, turn)
    return result


def local(field, gamma, kappa_zonal, kappa_merid, area, sea_mask, fold_pair):
    levels, height, width = field.shape
    lanes = levels * width
    devices_x, devices_y = lax.axis_size("lon"), lax.axis_size("lat")
    count = 2 * (width - 3).bit_length()
    operands = (field, gamma, kappa_zonal, kappa_merid, area, sea_mask, fold_pair)
    scratch = [pltpu.VMEM(x.shape, x.dtype) for x in operands[:-1]]
    scratch += [pltpu.SMEM(fold_pair.shape, fold_pair.dtype), pltpu.SemaphoreType.DMA((len(operands),))]
    if width == 2 * devices_x * devices_y and levels == 2 and devices_y * height == lanes == 4 * height:
        return local_by_columns(operands, scratch, count)
    message, payload, factors, keep, turn = run(
        block_local,
        [
            array(devices_x * devices_y, 4, lanes),
            array(5, height, lanes),
            array(count, height, lanes),
            array(4, height, lanes),
            array(devices_x, lanes, dtype=jnp.int32),
        ],
        *operands,
        outside=True,
        scratch=scratch,
    )
    ring_rows = lax.all_to_all(message, ("lon", "lat"), split_axis=0, concat_axis=0, tiled=True)
    ring_rows = ring_rows.reshape(devices_x, devices_y, 4, lanes)
    payload = lax.all_gather(payload, "lat", axis=0, tiled=False)
    kept, message = run(
        column_join,
        [array(2, height, lanes), array(devices_x, 2 * height + 8, lanes)],
        ring_rows, payload, keep,
    )
    gathered = lax.all_to_all(message, "lon", split_axis=0, concat_axis=0, tiled=True)
    (result,) = run(
        zonal_close, [array(levels, height, width)], gathered, ring_rows, kept, factors, keep, turn
    )
    return result


def solution(mesh):
    blocks = P(None, "lat", "lon")
    return jax.shard_map(
        local,
        mesh=mesh,
        in_specs=(blocks, blocks, blocks, blocks, P("lat", "lon"), P("lat", "lon"), P("lon")),
        out_specs=blocks,
        check_vma=False,
    )
```
